256 devices in a mesh: child: 8 (over x, core), row: 8 (over z), col: 4 (over y).
Axes of the slice: x: 4, y: 4, z: 8, core: 2. Of those that a mesh axis runs over, the one named last changes fastest.
Arguments:
- schur_blocks: bfloat16 [8, 8192, 8192], P('child', 'row', 'col'), may hold values from -0.0625 to 0.0625
- sketch_cols: bfloat16 [8192, 256], P('row'), may hold values from -6 to 6
- block_map: int32 [8, 64], replicated, may hold values from 0 to 255, as said below
- owner_slot: int32 [32], replicated, may hold values from 0 to 15, as said below
Outputs:
- basis_out: float32 [16, 8, 1024, 256], P('child', 'row', 'col')
- coupling_out: float32 [16, 8, 256, 256], P('child', 'row', 'col')
The draws below stay inside these ranges and needn't reach their ends.
Inputs may be any that keep to these rules, and one draw needn't show every extreme that they name: `block_map`: entry [c, j] keeps the block's place in its group (entry % 8 == j % 8) and lies at the row position of the child's group: (entry // 8) // 4 == (j // 8). The entries of one child are distinct. Of the blocks of one child with equal (j // 8), at most 4 land in groups whose owner_slot // 2 is equal, and in every draw exactly 4 do for one owner. Group g belongs to owner owner_slot[g] // 2. Groups with equal g // 4 have distinct slots, and at every row position some owner holds 2 groups.
All inputs are finite; a program needn't handle non-finite values.
Results may differ from the reference program's by a relative error of at most 0.017.
Values may be sent and summed in bfloat16 or wider, within the bound.
A program may use at most 64 MiB of HBM per device.

```python
import jax
import jax.numpy as jnp
from jax import lax

ORDER = 8192
SKETCH = 256
BLOCK = 128
GROUP = 1024
POSGROUPS = 4
SLOTS = 2
CHILDREN = 8
POSITIONS = 8
OFFSETS = 8
SPAN = 1
NBLOCKS = 64
PGROUPS = 32
PBLOCKS = 256
OWNSLOTS = 16


def permute_each(key, count, length):

    def single(subkey):
        return jax.random.permutation(subkey, length)
    return jax.vmap(single)(jax.random.split(key, count))


def parent_layout(key):
    positions = PGROUPS // POSGROUPS
    favoured = jax.random.randint(jax.random.fold_in(key, 101), (positions,), 0, CHILDREN)
    flipped = jax.random.randint(jax.random.fold_in(key, 102), (positions,), 0, 2)
    group_order = permute_each(jax.random.fold_in(key, 103), positions, POSGROUPS).astype(jnp.int32)
    others = permute_each(jax.random.fold_in(key, 104), positions, (CHILDREN - 1) * SLOTS)[:, :POSGROUPS - 2]
    other_owner = (favoured[:, None] + 1 + others // SLOTS) % CHILDREN
    other_slot = other_owner * SLOTS + others % SLOTS
    first_slot = favoured * SLOTS + flipped
    second_slot = favoured * SLOTS + 1 - flipped
    values = jnp.concatenate([first_slot[:, None], second_slot[:, None], other_slot], axis=1).astype(jnp.int32)
    index = jnp.arange(positions, dtype=jnp.int32)[:, None] * POSGROUPS + group_order
    owner_table = jnp.zeros((PGROUPS,), jnp.int32).at[index.reshape(-1)].set(values.reshape(-1))
    offset_order = permute_each(jax.random.fold_in(key, 105), CHILDREN * positions, OFFSETS).reshape(CHILDREN, positions, OFFSETS)
    offset_rank = jnp.argsort(offset_order, axis=-1)
    favoured_half = offset_rank < OFFSETS // 2
    flips = jax.random.randint(jax.random.fold_in(key, 106), (CHILDREN, positions, SPAN, OFFSETS), 0, 2)
    picked = (jnp.arange(SPAN, dtype=jnp.int32)[None, None, :, None] + flips) % 2
    order_grid = group_order[None, :, None, None, :]
    near_group = jnp.where(picked == 0, order_grid[..., 0], order_grid[..., 1])
    far_group = jnp.where(picked == 0, order_grid[..., 2], order_grid[..., 3])
    chosen = jnp.where(favoured_half[:, :, None, :], near_group, far_group)
    parent_group = jnp.arange(positions, dtype=jnp.int32)[None, :, None, None] * POSGROUPS + chosen
    blocks = parent_group * OFFSETS + jnp.arange(OFFSETS, dtype=jnp.int32)[None, None, None, :]
    return (blocks.reshape(CHILDREN, NBLOCKS).astype(jnp.int32), owner_table)


def draw_block_map(key, part):
    return parent_layout(key)[0]


def draw_owner_slot(key, part):
    return parent_layout(key)[1]


def shard_levels(rng, extent, pieces, low, top_value):
    gain, own = 1.0, jax.random.fold_in(rng, 6)
    for dim, parts in pieces:
        draws = jnp.exp(jax.random.uniform(jax.random.fold_in(own, dim), (parts,), jnp.float32, low / len(pieces), top_value / len(pieces)))
        gain = gain * jnp.repeat(draws, extent[dim] // parts).reshape([-1 if axis == dim else 1 for axis in range(len(extent))])
    return gain


def centred(rng, dims, spread, reach, shards=(), kind=jnp.bfloat16):
    level = shard_levels(rng, dims, shards, -0.22, 0.18) if shards else 1.0
    array = jax.random.normal(rng, dims, jnp.float32) * spread * level
    return jnp.minimum(jnp.maximum(array, -reach), reach).astype(kind)


def setup_inputs(seed: int = 0) -> dict:
    streams_of = jax.random.split(jax.random.key(seed), 5)
    return {
        "schur_blocks": centred(streams_of[0], (CHILDREN, ORDER, ORDER), ORDER ** -0.5, 0.0625, ((0, 8), (1, 8), (2, 4))),
        "sketch_cols": centred(streams_of[1], (ORDER, SKETCH), 1.0, 6.0, ((0, 8),)),
        "block_map": draw_block_map(jax.random.fold_in(streams_of[4], 71), 0),
        "owner_slot": draw_owner_slot(jax.random.fold_in(streams_of[4], 71), 0),
    }


gram_shift = 64.0

def orthonormal(parent_rows):
    gram_matrix = jnp.einsum('gnr,gnq->grq', parent_rows, parent_rows, precision=lax.Precision.HIGHEST)
    gram_matrix = gram_matrix + gram_shift * jnp.eye(SKETCH, dtype=jnp.float32)
    factor = jnp.linalg.cholesky(gram_matrix)
    solved = jax.scipy.linalg.solve_triangular(factor, jnp.swapaxes(parent_rows, 1, 2), lower=True)
    return jnp.swapaxes(solved, 1, 2)

def reference(schur_blocks, sketch_cols, block_map, owner_slot):
    offsets = GROUP // BLOCK
    samples = jnp.zeros((PBLOCKS, BLOCK, SKETCH), jnp.float32)
    for member in range(CHILDREN):
        matrix = schur_blocks[member]
        power_cols = lax.dot_general(matrix.astype(jnp.float32), sketch_cols.astype(jnp.float32), (((0,), (0,)), ((), ())), preferred_element_type=jnp.float32).astype(jnp.bfloat16)
        image_rows = jnp.dot(matrix.astype(jnp.float32), power_cols.astype(jnp.float32), preferred_element_type=jnp.float32)
        samples = samples.at[block_map[member]].add(image_rows.reshape(NBLOCKS, BLOCK, SKETCH))
    basis_rows = orthonormal(samples.reshape(PGROUPS, GROUP, SKETCH))
    rounded = basis_rows.astype(jnp.bfloat16).reshape(PBLOCKS, BLOCK, SKETCH)
    coupling = jnp.zeros((PGROUPS, SKETCH, SKETCH), jnp.float32)
    for member in range(CHILDREN):
        matrix = schur_blocks[member]
        child_basis = rounded[block_map[member]]
        weighted = jnp.dot(matrix.astype(jnp.float32), child_basis.reshape(ORDER, SKETCH).astype(jnp.float32), preferred_element_type=jnp.float32)
        projected = jnp.einsum('bxr,bxs->brs', child_basis.astype(jnp.float32), weighted.reshape(NBLOCKS, BLOCK, SKETCH), precision=lax.Precision.HIGHEST)
        coupling = coupling.at[block_map[member] // offsets].add(projected)
    position = jnp.arange(PGROUPS, dtype=jnp.int32) // POSGROUPS
    basis_out = jnp.zeros((OWNSLOTS, POSITIONS, GROUP, SKETCH), jnp.float32).at[owner_slot, position].set(basis_rows)
    coupling_out = jnp.zeros((OWNSLOTS, POSITIONS, SKETCH, SKETCH), jnp.float32).at[owner_slot, position].set(coupling)
    return (basis_out, coupling_out)
```

```python
import functools

import jax
import jax.numpy as jnp
from jax import lax
from jax.experimental import pallas as pl
from jax.experimental.pallas import tpu as pltpu
from jax.sharding import PartitionSpec as P

MESH = pl.DeviceIdType.MESH
F32, BF16 = jnp.float32, jnp.bfloat16
HIGHEST = lax.Precision.HIGHEST
VMEM_LIMIT = 60 * 1024 * 1024
SHIFT = 64.0


def ring(value, size):
    return lax.rem(value + 2 * size, size)


def dot(left, right, dims=((1,), (0,)), precision=None):
    return lax.dot_general(left, right, (dims, ((), ())), precision=precision, preferred_element_type=F32)


def greet(peers):
    barrier = pltpu.get_barrier_semaphore()
    for peer in peers:
        pl.semaphore_signal(barrier, inc=1, device_id=peer, device_id_type=MESH)
    pl.semaphore_wait(barrier, len(peers))


def send(source, target, send_sem, recv_sem, peer):
    copy = pltpu.make_async_remote_copy(
        src_ref=source,
        dst_ref=target,
        send_sem=send_sem,
        recv_sem=recv_sem,
        device_id=peer,
        device_id_type=MESH,
    )
    copy.start()
    return copy


def place():
    return lax.axis_index("child"), lax.axis_index("row"), lax.axis_index("col")


def columns(chunk):
    return pl.ds(pl.multiple_of(chunk * 256, 256), 256)


def hops_down(half):
    return 4 - half


def hops_up(half):
    return 3 + half


def sample_kernel(
    schur, sketch, block_map, own_out, gram_out,
    held, turned, part, sums_out, sums_in, power, total, b_out, b_in, c_out, c_in, z_all,
    load_sem, a_send, a_recv, p_send, p_recv, b_send, b_recv, c_send, c_recv, z_send, z_recv,
):
    c, r, k = place()
    pair, core = lax.div(c, 2), lax.rem(c, 2)
    below, above = {"row": ring(r - 1, 8)}, {"row": ring(r + 1, 8)}
    order = (4, 5, 3, 6, 2, 7, 1, 0)
    loads = {}
    for spot, rel in enumerate(order):
        chunk = ring(r + rel, 8)
        loads[rel] = pltpu.make_async_copy(schur.at[0, :, columns(chunk)], held.at[chunk], load_sem.at[spot])
        loads[rel].start()
    siblings = [{"child": ring(c + i, 8)} for i in range(1, 8)]
    group = [{"col": ring(k + i, 4)} for i in range(1, 4)]
    cross = [{"child": 2 * pair + 1 - core, "col": ring(k + i, 4)} for i in range(1, 4)]
    greet([below, above] + siblings + group + cross)
    turned[...] = sketch[...].T

    def produce(rel):
        chunk = ring(r + rel, 8)
        loads[rel].wait()
        part[chunk] = dot(turned[...], held[chunk])

    pending = []
    arriving = {}

    def pass_on(way, half, step):
        hops = hops_down(half) if way == 0 else hops_up(half)
        if step >= hops:
            return
        chunk = ring(r - hops + step if way == 0 else r + hops - step, 8)
        value = part[chunk, pl.ds(128 * half, 128)]
        if step:
            arriving[way, half, step - 1].wait_recv()
            value = value + sums_in[way, half, step - 1].astype(F32)
        sums_out[way, half, step] = value.astype(BF16)
        copy = send(
            sums_out.at[way, half, step], sums_in.at[way, half, step],
            a_send.at[way, half, step], a_recv.at[way, half, step], below if way == 0 else above,
        )
        arriving[way, half, step] = copy
        pending.append(copy)

    produce(4)
    pass_on(0, 0, 0)
    pass_on(1, 1, 0)
    produce(5)
    pass_on(0, 1, 0)
    produce(3)
    pass_on(1, 0, 0)
    for step, rels in ((1, (6, 2)), (2, (7, 1)), (3, (0,))):
        for rel in rels:
            produce(rel)
        for way, half in ((0, 0), (1, 1), (0, 1), (1, 0)):
            pass_on(way, half, step)
    for half in range(2):
        value = part[r, pl.ds(128 * half, 128)]
        for way, hops in ((0, hops_down(half)), (1, hops_up(half))):
            arriving[way, half, hops - 1].wait_recv()
            value = value + sums_in[way, half, hops - 1].astype(F32)
        power[r, pl.ds(128 * half, 128)] = value.astype(BF16)

    coming = {}

    def share(way, half, step):
        hops = 4 - half if way == 0 else 3 + half
        if step >= hops:
            return
        chunk = ring(r - step if way == 0 else r + step, 8)
        if step:
            coming[way, half, step - 1].wait_recv()
        ref = power.at[chunk, pl.ds(128 * half, 128)]
        copy = send(ref, ref, p_send.at[way, half, step], p_recv.at[way, half, step], above if way == 0 else below)
        coming[way, half, step] = copy
        pending.append(copy)

    def multiply(chunk):
        return dot(held[chunk], power[chunk], ((1,), (1,)))

    for step in range(4):
        for way in range(2):
            for half in range(2):
                share(way, half, step)
        if step == 0:
            total[...] = multiply(r)
            continue
        if step == 3:
            coming[0, 1, 2].wait_recv()
            coming[1, 0, 2].wait_recv()
        total[...] += multiply(ring(r - step, 8))
        total[...] += multiply(ring(r + step, 8))
    coming[0, 0, 3].wait_recv()
    coming[1, 1, 3].wait_recv()
    last = ring(r + 4, 8)
    copies = []
    for i in (2, 1, 3, 0):
        peer = ring(k + i, 4)
        rows = pl.ds(pl.multiple_of(peer * 256, 256), 256)
        value = total[rows] + dot(held[last, rows], power[last], ((1,), (1,)))
        if i:
            b_out[i - 1] = value.astype(BF16)
            copies.append(send(b_out.at[i - 1], b_in.at[i - 1], b_send.at[i - 1], b_recv.at[i - 1], {"col": peer}))
        else:
            summed = value
    for copy, i in zip(copies, (2, 1, 3)):
        copy.wait_recv()
        summed = summed + b_in[i - 1].astype(F32)
    pending += copies
    c_out[...] = summed.astype(BF16).reshape(2, 128, 256)

    copies = []
    for i in (4, 3, 5, 2, 6, 1, 7):
        peer = ring(c + i, 8)
        copies.append(send(c_out.at[lax.rem(peer, 2)], c_in.at[c], c_send.at[i - 1], c_recv.at[i - 1], {"child": peer}))
    c_in[c] = c_out[core]
    for copy in copies:
        copy.wait_recv()
    pending += copies
    spot = 8 * r + 2 * k + core
    value = jnp.zeros((128, 256), F32)
    for child in range(8):
        wanted = lax.shift_right_logical(block_map[child, spot], 3) == 4 * r + pair
        value = value + c_in[child].astype(F32) * jnp.where(wanted, 1.0, 0.0)
    own_out[...] = value
    offset = 2 * k + core
    z_all[offset] = value.astype(BF16)
    copies = []
    ref = z_all.at[offset]
    for i in (2, 1, 3, 0):
        peer = ring(k + i, 4)
        for other in range(2):
            if i == 0 and other == 0:
                continue
            slot = 2 * i + other - 1
            copies.append(send(ref, ref, z_send.at[slot], z_recv.at[slot],
                               {"child": c if other == 0 else 2 * pair + 1 - core, "col": peer}))
    for copy in copies:
        copy.wait_recv()
    pending += copies
    rows = z_all[...].reshape(1024, 256)
    gram_out[...] = dot(rows, rows, ((0,), (0,)))
    for copy in pending:
        copy.wait_send()


def coupling_kernel(
    schur, basis, block_map, owner_slot, basis_out, coupling_out,
    held, e_in, mine, column_in, row_in, total, sums, f_out, f_in, g_out, g_in, h_out, h_in,
    load_sem, e_send, e_recv, z_send, z_recv, y_send, y_recv, r_send, r_recv, f_send, f_recv, g_send, g_recv,
    h_send, h_recv,
):
    c, r, k = place()
    below, above = {"row": ring(r - 1, 8)}, {"row": ring(r + 1, 8)}
    loads = []
    for chunk in range(8):
        loads.append(pltpu.make_async_copy(schur.at[0, :, columns(chunk)], held.at[chunk], load_sem.at[chunk]))
        loads[-1].start()
    siblings = [{"child": ring(c + i, 8)} for i in range(1, 8)]
    greet([below, above] + siblings + [{"col": ring(k + i, 4)} for i in range(1, 4)])
    pending = []

    copies = []
    for i in (4, 3, 5, 2, 6, 1, 7):
        copies.append(send(basis, e_in.at[c], e_send.at[i - 1], e_recv.at[i - 1], {"child": ring(c + i, 8)}))
    e_in[c] = basis[...]
    for copy in copies:
        copy.wait_recv()
    pending += copies
    for half in range(2):
        near = lax.rem(lax.shift_right_logical(block_map[c, 8 * r + 2 * k + half], 3), 4)
        mine[r, pl.ds(128 * half, 128)] = e_in[2 * near + half]

    arriving = {}
    forwards = []

    def share(way, half, step):
        hops = 4 - half if way == 0 else 3 + half
        if step:
            arriving[way, half, step - 1].wait_recv()
        if step >= hops:
            return
        chunk = ring(r - step if way == 0 else r + step, 8)
        ref = mine.at[chunk, pl.ds(128 * half, 128)]
        copy = send(ref, ref, z_send.at[way, half, step], z_recv.at[way, half, step], above if way == 0 else below)
        arriving[way, half, step] = copy
        pending.append(copy)

    def across(rel, half):
        chunk = ring(r + rel, 8)
        peer = lax.div(chunk, 2)
        copy = pltpu.make_async_remote_copy(
            src_ref=mine.at[chunk, pl.ds(128 * half, 128)],
            dst_ref=column_in.at[lax.rem(chunk, 2), k, pl.ds(128 * half, 128)],
            send_sem=y_send.at[rel, half],
            recv_sem=y_recv.at[lax.rem(chunk, 2), k, half],
            device_id={"col": peer},
            device_id_type=MESH,
        )
        pl.when(peer != k)(copy.start)
        forwards.append((peer, copy))

    row_copies = []
    for half in range(2):
        share(0, half, 0)
        share(1, half, 0)
    for half in range(2):
        across(0, half)
    for i in (2, 1, 3):
        row_copies.append(send(mine.at[r], row_in.at[k], r_send.at[i - 1], r_recv.at[i - 1], {"col": ring(k + i, 4)}))
    row_in[k] = mine[r]

    for slot in range(2):
        for half in range(2):
            value = jnp.zeros((128, 256), F32)
            for g in range(4):
                wanted = owner_slot[4 * r + g] == 2 * c + slot
                value = value + e_in[2 * g + half].astype(F32) * jnp.where(wanted, 1.0, 0.0)
            basis_out[slot, 0, pl.ds(128 * half, 128)] = value

    for step in range(1, 5):
        for way, half in ((0, 0), (1, 1), (0, 1), (1, 0)):
            hops = 4 - half if way == 0 else 3 + half
            if step > hops:
                continue
            share(way, half, step)
            across((8 - step if way == 0 else step) % 8, half)
    for load in loads:
        load.wait()
    total[...] = dot(held[k], mine[2 * k]) + dot(held[4 + k], mine[2 * k + 1])
    for i in (1, 3, 2):
        peer = ring(k + i, 4)
        for odd in range(2):
            for half in range(2):
                pltpu.make_async_remote_copy(
                    src_ref=mine.at[0, pl.ds(128 * half, 128)],
                    dst_ref=column_in.at[odd, peer, pl.ds(128 * half, 128)],
                    send_sem=y_send.at[0, half],
                    recv_sem=y_recv.at[odd, peer, half],
                    device_id={"col": peer},
                    device_id_type=MESH,
                ).wait_recv()
            total[...] += dot(held[4 * odd + peer], column_in[odd, peer])
    for copy in row_copies:
        copy.wait_recv()
    pending += row_copies

    sums[...] = jnp.zeros_like(sums)
    for offset in range(8):
        value = total[pl.ds(128 * offset, 128)]
        high = value.astype(BF16)
        low = (value - high.astype(F32)).astype(BF16)
        left = row_in[offset // 2, pl.ds(128 * (offset % 2), 128)]
        product = dot(left, high, ((0,), (0,))) + dot(left, low, ((0,), (0,)))
        near = lax.rem(lax.shift_right_logical(block_map[c, 8 * r + offset], 3), 4)
        for g in range(4):
            sums[g] += product * jnp.where(near == g, 1.0, 0.0)

    copies = []
    for i in (2, 1, 3):
        peer = ring(k + i, 4)
        rows = pl.ds(pl.multiple_of(peer * 64, 64), 64)
        f_out[i - 1] = sums[:, rows].astype(BF16)
        copies.append(send(f_out.at[i - 1], f_in.at[i - 1], f_send.at[i - 1], f_recv.at[i - 1], {"col": peer}))
    value = sums[:, pl.ds(pl.multiple_of(k * 64, 64), 64)]
    for copy, i in zip(copies, (2, 1, 3)):
        copy.wait_recv()
        value = value + f_in[i - 1].astype(F32)
    pending += copies
    g_out[...] = value.astype(BF16).reshape(8, 32, 256)
    copies = []
    for i in (4, 3, 5, 2, 6, 1, 7):
        peer = ring(c + i, 8)
        copies.append(send(g_out.at[peer], g_in.at[c], g_send.at[i - 1], g_recv.at[i - 1], {"child": peer}))
    g_in[c] = g_out[c]
    for copy in copies:
        copy.wait_recv()
    pending += copies
    h_out[...] = jnp.sum(g_in[...].astype(F32), axis=0).astype(BF16)
    copies = []
    for i in (4, 3, 5, 2, 6, 1, 7):
        copies.append(send(h_out, h_in.at[c], h_send.at[i - 1], h_recv.at[i - 1], {"child": ring(c + i, 8)}))
    h_in[c] = h_out[...]
    for copy in copies:
        copy.wait_recv()
    pending += copies
    for slot in range(2):
        for half in range(2):
            value = jnp.zeros((32, 256), F32)
            for g in range(4):
                wanted = owner_slot[4 * r + g] == 2 * c + slot
                value = value + h_in[2 * g + half].astype(F32) * jnp.where(wanted, 1.0, 0.0)
            coupling_out[slot, 0, pl.ds(32 * half, 32)] = value
    for copy in pending:
        copy.wait_send()
    for peer, copy in forwards:
        pl.when(peer != k)(copy.wait_send)


def orthonormal(own, gram):
    factor = jnp.linalg.cholesky(gram + SHIFT * jnp.eye(256, dtype=F32))
    return jax.scipy.linalg.solve_triangular(factor, own.T, lower=True).T


def in_vmem():
    return pl.BlockSpec(memory_space=pltpu.VMEM)


def in_smem():
    return pl.BlockSpec(memory_space=pltpu.SMEM)


def sampled(schur, sketch, block_map):
    dma = pltpu.SemaphoreType.DMA
    return pl.pallas_call(
        sample_kernel,
        out_shape=(jax.ShapeDtypeStruct((128, 256), F32), jax.ShapeDtypeStruct((256, 256), F32)),
        in_specs=[pl.BlockSpec(memory_space=pl.ANY), in_vmem(), in_smem()],
        out_specs=(in_vmem(), in_vmem()),
        scratch_shapes=[
            pltpu.VMEM((8, 1024, 256), BF16),
            pltpu.VMEM((256, 1024), BF16),
            pltpu.VMEM((8, 256, 256), F32),
            pltpu.VMEM((2, 2, 4, 128, 256), BF16),
            pltpu.VMEM((2, 2, 4, 128, 256), BF16),
            pltpu.VMEM((8, 256, 256), BF16),
            pltpu.VMEM((1024, 256), F32),
            pltpu.VMEM((3, 256, 256), BF16),
            pltpu.VMEM((3, 256, 256), BF16),
            pltpu.VMEM((2, 128, 256), BF16),
            pltpu.VMEM((8, 128, 256), BF16),
            pltpu.VMEM((8, 128, 256), BF16),
            dma((8,)),
            dma((2, 2, 4)), dma((2, 2, 4)),
            dma((2, 2, 4)), dma((2, 2, 4)),
            dma((3,)), dma((3,)),
            dma((7,)), dma((7,)),
            dma((8,)), dma((8,)),
        ],
        compiler_params=pltpu.CompilerParams(
            collective_id=0, has_side_effects=True, vmem_limit_bytes=VMEM_LIMIT
        ),
        name="samples",
    )(schur, sketch, block_map)


def coupled(schur, basis, block_map, owner_slot):
    dma = pltpu.SemaphoreType.DMA
    return pl.pallas_call(
        coupling_kernel,
        out_shape=(
            jax.ShapeDtypeStruct((2, 1, 256, 256), F32),
            jax.ShapeDtypeStruct((2, 1, 64, 256), F32),
        ),
        in_specs=[pl.BlockSpec(memory_space=pl.ANY), in_vmem(), in_smem(), in_smem()],
        out_specs=(in_vmem(), in_vmem()),
        scratch_shapes=[
            pltpu.VMEM((8, 1024, 256), BF16),
            pltpu.VMEM((8, 128, 256), BF16),
            pltpu.VMEM((8, 256, 256), BF16),
            pltpu.VMEM((2, 4, 256, 256), BF16),
            pltpu.VMEM((4, 256, 256), BF16),
            pltpu.VMEM((1024, 256), F32),
            pltpu.VMEM((4, 256, 256), F32),
            pltpu.VMEM((3, 4, 64, 256), BF16),
            pltpu.VMEM((3, 4, 64, 256), BF16),
            pltpu.VMEM((8, 32, 256), BF16),
            pltpu.VMEM((8, 32, 256), BF16),
            pltpu.VMEM((32, 256), BF16),
            pltpu.VMEM((8, 32, 256), BF16),
            dma((8,)),
            dma((7,)), dma((7,)),
            dma((2, 2, 4)), dma((2, 2, 4)),
            dma((8, 2)), dma((2, 4, 2)),
            dma((3,)), dma((3,)),
            dma((3,)), dma((3,)),
            dma((7,)), dma((7,)),
            dma((7,)), dma((7,)),
        ],
        compiler_params=pltpu.CompilerParams(
            collective_id=1, has_side_effects=True, vmem_limit_bytes=VMEM_LIMIT
        ),
        name="coupling",
    )(schur, basis, block_map, owner_slot)


def shards(schur_blocks, sketch_cols, block_map, owner_slot):
    own, gram = sampled(schur_blocks, sketch_cols, block_map)
    basis = orthonormal(own, gram)
    return coupled(schur_blocks, basis.astype(BF16), block_map, owner_slot)


def solution(mesh):
    placed = (P("child", "row", "col"), P("row", None), P(), P())
    return jax.shard_map(
        shards,
        mesh=mesh,
        in_specs=placed,
        out_specs=(P("child", "row", "col", None), P("child", "row", "col", None)),
        check_vma=False,
    )
```

```python
import functools

import jax
import jax.numpy as jnp
from jax import lax
from jax.experimental import pallas as pl
from jax.experimental.pallas import tpu as pltpu
from jax.sharding import PartitionSpec as P

MESH = pl.DeviceIdType.MESH
F32, BF16 = jnp.float32, jnp.bfloat16
HIGHEST = lax.Precision.HIGHEST
VMEM_LIMIT = 60 * 1024 * 1024
SHIFT = 64.0


def ring(value, size):
    return lax.rem(value + 2 * size, size)


def dot(left, right, dims=((1,), (0,)), precision=None):
    return lax.dot_general(left, right, (dims, ((), ())), precision=precision, preferred_element_type=F32)


def greet(peers):
    barrier = pltpu.get_barrier_semaphore()
    for peer in peers:
        pl.semaphore_signal(barrier, inc=1, device_id=peer, device_id_type=MESH)
    pl.semaphore_wait(barrier, len(peers))


def send(source, target, send_sem, recv_sem, peer):
    copy = pltpu.make_async_remote_copy(
        src_ref=source,
        dst_ref=target,
        send_sem=send_sem,
        recv_sem=recv_sem,
        device_id=peer,
        device_id_type=MESH,
    )
    copy.start()
    return copy


def place():
    return lax.axis_index("child"), lax.axis_index("row"), lax.axis_index("col")


def columns(chunk):
    return pl.ds(pl.multiple_of(chunk * 256, 256), 256)


def hops_down(half):
    return 4 - half


def hops_up(half):
    return 3 + half


def sample_kernel(
    schur, sketch, block_map, own_out, gram_out,
    held, turned, part, sums_out, sums_in, power, total, b_out, b_in, c_out, c_in, z_all,
    load_sem, a_send, a_recv, p_send, p_recv, b_send, b_recv, c_send, c_recv, z_send, z_recv,
):
    c, r, k = place()
    pair, core = lax.div(c, 2), lax.rem(c, 2)
    below, above = {"row": ring(r - 1, 8)}, {"row": ring(r + 1, 8)}
    order = (4, 5, 3, 6, 2, 7, 1, 0)
    loads = {}
    for spot, rel in enumerate(order):
        chunk = ring(r + rel, 8)
        loads[rel] = pltpu.make_async_copy(schur.at[0, :, columns(chunk)], held.at[chunk], load_sem.at[spot])
        loads[rel].start()
    siblings = [{"child": ring(c + i, 8)} for i in range(1, 8)]
    group = [{"col": ring(k + i, 4)} for i in range(1, 4)]
    cross = [{"child": 2 * pair + 1 - core, "col": ring(k + i, 4)} for i in range(1, 4)]
    greet([below, above] + siblings + group + cross)
    turned[...] = sketch[...].T

    def produce(rel):
        chunk = ring(r + rel, 8)
        loads[rel].wait()
        part[chunk] = dot(turned[...], held[chunk])

    pending = []
    arriving = {}

    def pass_on(way, half, step):
        hops = hops_down(half) if way == 0 else hops_up(half)
        if step >= hops:
            return
        chunk = ring(r - hops + step if way == 0 else r + hops - step, 8)
        value = part[chunk, pl.ds(128 * half, 128)]
        if step:
            arriving[way, half, step - 1].wait_recv()
            value = value + sums_in[way, half, step - 1].astype(F32)
        sums_out[way, half, step] = value.astype(BF16)
        copy = send(
            sums_out.at[way, half, step], sums_in.at[way, half, step],
            a_send.at[way, half, step], a_recv.at[way, half, step], below if way == 0 else above,
        )
        arriving[way, half, step] = copy
        pending.append(copy)

    produce(4)
    pass_on(0, 0, 0)
    pass_on(1, 1, 0)
    produce(5)
    pass_on(0, 1, 0)
    produce(3)
    pass_on(1, 0, 0)
    for step, rels in ((1, (6, 2)), (2, (7, 1)), (3, (0,))):
        for rel in rels:
            produce(rel)
        for way, half in ((0, 0), (1, 1), (0, 1), (1, 0)):
            pass_on(way, half, step)
    for half in range(2):
        value = part[r, pl.ds(128 * half, 128)]
        for way, hops in ((0, hops_down(half)), (1, hops_up(half))):
            arriving[way, half, hops - 1].wait_recv()
            value = value + sums_in[way, half, hops - 1].astype(F32)
        power[r, pl.ds(128 * half, 128)] = value.astype(BF16)

    coming = {}

    def share(way, half, step):
        hops = 4 - half if way == 0 else 3 + half
        if step >= hops:
            return
        chunk = ring(r - step if way == 0 else r + step, 8)
        if step:
            coming[way, half, step - 1].wait_recv()
        ref = power.at[chunk, pl.ds(128 * half, 128)]
        copy = send(ref, ref, p_send.at[way, half, step], p_recv.at[way, half, step], above if way == 0 else below)
        coming[way, half, step] = copy
        pending.append(copy)

    def multiply(chunk):
        return dot(held[chunk], power[chunk], ((1,), (1,)))

    for step in range(4):
        for way in range(2):
            for half in range(2):
                share(way, half, step)
        if step == 0:
            total[...] = multiply(r)
            continue
        if step == 3:
            coming[0, 1, 2].wait_recv()
            coming[1, 0, 2].wait_recv()
        total[...] += multiply(ring(r - step, 8))
        total[...] += multiply(ring(r + step, 8))
    coming[0, 0, 3].wait_recv()
    coming[1, 1, 3].wait_recv()
    last = ring(r + 4, 8)
    copies = []
    for i in (2, 1, 3, 0):
        peer = ring(k + i, 4)
        rows = pl.ds(pl.multiple_of(peer * 256, 256), 256)
        value = total[rows] + dot(held[last, rows], power[last], ((1,), (1,)))
        if i:
            b_out[i - 1] = value.astype(BF16)
            copies.append(send(b_out.at[i - 1], b_in.at[i - 1], b_send.at[i - 1], b_recv.at[i - 1], {"col": peer}))
        else:
            summed = value
    for copy, i in zip(copies, (2, 1, 3)):
        copy.wait_recv()
        summed = summed + b_in[i - 1].astype(F32)
    pending += copies
    c_out[...] = summed.astype(BF16).reshape(2, 128, 256)

    copies = []
    for i in (4, 3, 5, 2, 6, 1, 7):
        peer = ring(c + i, 8)
        copies.append(send(c_out.at[lax.rem(peer, 2)], c_in.at[c], c_send.at[i - 1], c_recv.at[i - 1], {"child": peer}))
    c_in[c] = c_out[core]
    for copy in copies:
        copy.wait_recv()
    pending += copies
    spot = 8 * r + 2 * k + core
    value = jnp.zeros((128, 256), F32)
    for child in range(8):
        wanted = lax.shift_right_logical(block_map[child, spot], 3) == 4 * r + pair
        value = value + c_in[child].astype(F32) * jnp.where(wanted, 1.0, 0.0)
    own_out[...] = value
    offset = 2 * k + core
    z_all[offset] = value.astype(BF16)
    copies = []
    ref = z_all.at[offset]
    for i in (2, 1, 3, 0):
        peer = ring(k + i, 4)
        for other in range(2):
            if i == 0 and other == 0:
                continue
            slot = 2 * i + other - 1
            copies.append(send(ref, ref, z_send.at[slot], z_recv.at[slot],
                               {"child": c if other == 0 else 2 * pair + 1 - core, "col": peer}))
    for copy in copies:
        copy.wait_recv()
    pending += copies
    rows = z_all[...].reshape(1024, 256)
    gram_out[...] = dot(rows, rows, ((0,), (0,)))
    for copy in pending:
        copy.wait_send()


def coupling_kernel(
    schur, basis, block_map, owner_slot, basis_out, coupling_out,
    held, e_in, mine, column_in, row_in, total, sums, f_out, f_in, g_out, g_in, h_out, h_in,
    load_sem, e_send, e_recv, z_send, z_recv, y_send, y_recv, r_send, r_recv, f_send, f_recv, g_send, g_recv,
    h_send, h_recv,
):
    c, r, k = place()
    below, above = {"row": ring(r - 1, 8)}, {"row": ring(r + 1, 8)}
    loads = []
    for chunk in range(8):
        loads.append(pltpu.make_async_copy(schur.at[0, :, columns(chunk)], held.at[chunk], load_sem.at[chunk]))
        loads[-1].start()
    siblings = [{"child": ring(c + i, 8)} for i in range(1, 8)]
    greet([below, above] + siblings + [{"col": ring(k + i, 4)} for i in range(1, 4)])
    pending = []

    copies = []
    for i in (4, 3, 5, 2, 6, 1, 7):
        copies.append(send(basis, e_in.at[c], e_send.at[i - 1], e_recv.at[i - 1], {"child": ring(c + i, 8)}))
    e_in[c] = basis[...]
    for copy in copies:
        copy.wait_recv()
    pending += copies
    for half in range(2):
        near = lax.rem(lax.shift_right_logical(block_map[c, 8 * r + 2 * k + half], 3), 4)
        mine[r, pl.ds(128 * half, 128)] = e_in[2 * near + half]

    arriving = {}
    forwards = []

    def share(way, half, step):
        hops = 4 - half if way == 0 else 3 + half
        if step:
            arriving[way, half, step - 1].wait_recv()
        if step >= hops:
            return
        chunk = ring(r - step if way == 0 else r + step, 8)
        ref = mine.at[chunk, pl.ds(128 * half, 128)]
        copy = send(ref, ref, z_send.at[way, half, step], z_recv.at[way, half, step], above if way == 0 else below)
        arriving[way, half, step] = copy
        pending.append(copy)

    def across(rel, half):
        chunk = ring(r + rel, 8)
        peer = lax.div(chunk, 2)
        copy = pltpu.make_async_remote_copy(
            src_ref=mine.at[chunk, pl.ds(128 * half, 128)],
            dst_ref=column_in.at[lax.rem(chunk, 2), k, pl.ds(128 * half, 128)],
            send_sem=y_send.at[rel, half],
            recv_sem=y_recv.at[lax.rem(chunk, 2), k, half],
            device_id={"col": peer},
            device_id_type=MESH,
        )
        pl.when(peer != k)(copy.start)
        forwards.append((peer, copy))

    row_copies = []
    for half in range(2):
        share(0, half, 0)
        share(1, half, 0)
    for half in range(2):
        across(0, half)
    for i in (2, 1, 3):
        row_copies.append(send(mine.at[r], row_in.at[k], r_send.at[i - 1], r_recv.at[i - 1], {"col": ring(k + i, 4)}))
    row_in[k] = mine[r]

    for slot in range(2):
        for half in range(2):
            value = jnp.zeros((128, 256), F32)
            for g in range(4):
                wanted = owner_slot[4 * r + g] == 2 * c + slot
                value = value + e_in[2 * g + half].astype(F32) * jnp.where(wanted, 1.0, 0.0)
            basis_out[slot, 0, pl.ds(128 * half, 128)] = value

    for step in range(1, 5):
        for way, half in ((0, 0), (1, 1), (0, 1), (1, 0)):
            hops = 4 - half if way == 0 else 3 + half
            if step > hops:
                continue
            share(way, half, step)
            across((8 - step if way == 0 else step) % 8, half)
    for load in loads:
        load.wait()
    total[...] = dot(held[k], mine[2 * k]) + dot(held[4 + k], mine[2 * k + 1])
    for i in (1, 3, 2):
        peer = ring(k + i, 4)
        for odd in range(2):
            for half in range(2):
                pltpu.make_async_remote_copy(
                    src_ref=mine.at[0, pl.ds(128 * half, 128)],
                    dst_ref=column_in.at[odd, peer, pl.ds(128 * half, 128)],
                    send_sem=y_send.at[0, half],
                    recv_sem=y_recv.at[odd, peer, half],
                    device_id={"col": peer},
                    device_id_type=MESH,
                ).wait_recv()
            total[...] += dot(held[4 * odd + peer], column_in[odd, peer])
    for copy in row_copies:
        copy.wait_recv()
    pending += row_copies

    sums[...] = jnp.zeros_like(sums)
    for offset in range(8):
        value = total[pl.ds(128 * offset, 128)]
        high = value.astype(BF16)
        low = (value - high.astype(F32)).astype(BF16)
        left = row_in[offset // 2, pl.ds(128 * (offset % 2), 128)]
        product = dot(left, high, ((0,), (0,))) + dot(left, low, ((0,), (0,)))
        near = lax.rem(lax.shift_right_logical(block_map[c, 8 * r + offset], 3), 4)
        for g in range(4):
            sums[g] += product * jnp.where(near == g, 1.0, 0.0)

    copies = []
    for i in (2, 1, 3):
        peer = ring(k + i, 4)
        rows = pl.ds(pl.multiple_of(peer * 64, 64), 64)
        f_out[i - 1] = sums[:, rows].astype(BF16)
        copies.append(send(f_out.at[i - 1], f_in.at[i - 1], f_send.at[i - 1], f_recv.at[i - 1], {"col": peer}))
    value = sums[:, pl.ds(pl.multiple_of(k * 64, 64), 64)]
    for copy, i in zip(copies, (2, 1, 3)):
        copy.wait_recv()
        value = value + f_in[i - 1].astype(F32)
    pending += copies
    g_out[...] = value.astype(BF16).reshape(8, 32, 256)
    copies = []
    for i in (4, 3, 5, 2, 6, 1, 7):
        peer = ring(c + i, 8)
        copies.append(send(g_out.at[peer], g_in.at[c], g_send.at[i - 1], g_recv.at[i - 1], {"child": peer}))
    g_in[c] = g_out[c]
    for copy in copies:
        copy.wait_recv()
    pending += copies
    h_out[...] = jnp.sum(g_in[...].astype(F32), axis=0).astype(BF16)
    copies = []
    for i in (4, 3, 5, 2, 6, 1, 7):
        copies.append(send(h_out, h_in.at[c], h_send.at[i - 1], h_recv.at[i - 1], {"child": ring(c + i, 8)}))
    h_in[c] = h_out[...]
    for copy in copies:
        copy.wait_recv()
    pending += copies
    for slot in range(2):
        for half in range(2):
            value = jnp.zeros((32, 256), F32)
            for g in range(4):
                wanted = owner_slot[4 * r + g] == 2 * c + slot
                value = value + h_in[2 * g + half].astype(F32) * jnp.where(wanted, 1.0, 0.0)
            coupling_out[slot, 0, pl.ds(32 * half, 32)] = value
    for copy in pending:
        copy.wait_send()
    for peer, copy in forwards:
        pl.when(peer != k)(copy.wait_send)


def lanes(value, column):
    return jnp.broadcast_to(value[:, column : column + 1], (8, 128))


def sublanes(value, row):
    return jnp.broadcast_to(value[row : row + 1, :], (8, 128))


def inverse_factor(rows, marks):
    sub = lax.broadcasted_iota(jnp.int32, (8, 128), 0)
    for i in range(16):
        left = [[lanes(rows[t], 8 * i + p) for p in range(8)] for t in range(i, 16)]
        inner = {(q, p): sublanes(left[0][p], q) for p in range(8) for q in range(p, 8)}
        upper = [sublanes(rows[i], p) for p in range(8)]
        done = [sublanes(marks[i], p) for p in range(8)]
        for p in range(8):
            scale = lax.rsqrt(inner[p, p])
            for q in range(p + 1, 8):
                inner[q, p] = inner[q, p] * scale
            upper[p] = upper[p] * scale
            done[p] = done[p] * scale
            for t in range(1, 16 - i):
                left[t][p] = left[t][p] * scale
            for q in range(p + 1, 8):
                for s in range(q, 8):
                    inner[s, q] = inner[s, q] - inner[s, p] * inner[q, p]
                upper[q] = upper[q] - inner[q, p] * upper[p]
                done[q] = done[q] - inner[q, p] * done[p]
                for t in range(1, 16 - i):
                    left[t][q] = left[t][q] - left[t][p] * inner[q, p]
        for t in range(1, 16 - i):
            for p in range(8):
                if i + 1 < 16:
                    rows[i + t] = rows[i + t] - left[t][p] * upper[p]
                marks[i + t] = marks[i + t] - left[t][p] * done[p]
        value = done[0]
        for p in range(1, 8):
            value = jnp.where(sub == p, done[p], value)
        marks[i] = value
    return marks


def basis_kernel(own, gram, out, work, inverse, below):
    row = lax.broadcasted_iota(jnp.int32, (128, 128), 0)
    column = lax.broadcasted_iota(jnp.int32, (128, 128), 1)
    work[...] = gram[:128, :128] + jnp.where(row == column, SHIFT, 0.0)

    def step(part, carry):
        rows = [work[pl.ds(8 * t, 8)] for t in range(16)]
        sub = lax.broadcasted_iota(jnp.int32, (8, 128), 0)
        lane = lax.broadcasted_iota(jnp.int32, (8, 128), 1)
        marks = [jnp.where(lane == sub + 8 * t, 1.0, 0.0) for t in range(16)]
        marks = inverse_factor(rows, marks)
        for t in range(16):
            inverse[part, pl.ds(8 * t, 8)] = marks[t]

        @pl.when(part == 0)
        def _():
            below[...] = dot(gram[128:, :128], inverse[0], ((1,), (1,)), HIGHEST)
            work[...] = (
                gram[128:, 128:] + jnp.where(row == column, SHIFT, 0.0)
                - dot(below[...], below[...], ((1,), (1,)), HIGHEST)
            )
        return carry

    lax.fori_loop(0, 2, step, 0)
    first = dot(own[:, :128], inverse[0], ((1,), (1,)), HIGHEST)
    out[:, :128] = first.astype(BF16)
    rest = own[:, 128:] - dot(first, below[...], ((1,), (1,)), HIGHEST)
    out[:, 128:] = dot(rest, inverse[1], ((1,), (1,)), HIGHEST).astype(BF16)


def in_vmem():
    return pl.BlockSpec(memory_space=pltpu.VMEM)


def orthonormal(own, gram):
    return pl.pallas_call(
        basis_kernel,
        out_shape=jax.ShapeDtypeStruct((128, 256), BF16),
        in_specs=[in_vmem(), in_vmem()],
        out_specs=in_vmem(),
        scratch_shapes=[
            pltpu.VMEM((128, 128), F32),
            pltpu.VMEM((2, 128, 128), F32),
            pltpu.VMEM((128, 128), F32),
        ],
        name="basis",
    )(own, gram)


def in_smem():
    return pl.BlockSpec(memory_space=pltpu.SMEM)


def sampled(schur, sketch, block_map):
    dma = pltpu.SemaphoreType.DMA
    return pl.pallas_call(
        sample_kernel,
        out_shape=(jax.ShapeDtypeStruct((128, 256), F32), jax.ShapeDtypeStruct((256, 256), F32)),
        in_specs=[pl.BlockSpec(memory_space=pl.ANY), in_vmem(), in_smem()],
        out_specs=(in_vmem(), in_vmem()),
        scratch_shapes=[
            pltpu.VMEM((8, 1024, 256), BF16),
            pltpu.VMEM((256, 1024), BF16),
            pltpu.VMEM((8, 256, 256), F32),
            pltpu.VMEM((2, 2, 4, 128, 256), BF16),
            pltpu.VMEM((2, 2, 4, 128, 256), BF16),
            pltpu.VMEM((8, 256, 256), BF16),
            pltpu.VMEM((1024, 256), F32),
            pltpu.VMEM((3, 256, 256), BF16),
            pltpu.VMEM((3, 256, 256), BF16),
            pltpu.VMEM((2, 128, 256), BF16),
            pltpu.VMEM((8, 128, 256), BF16),
            pltpu.VMEM((8, 128, 256), BF16),
            dma((8,)),
            dma((2, 2, 4)), dma((2, 2, 4)),
            dma((2, 2, 4)), dma((2, 2, 4)),
            dma((3,)), dma((3,)),
            dma((7,)), dma((7,)),
            dma((8,)), dma((8,)),
        ],
        compiler_params=pltpu.CompilerParams(
            collective_id=0, has_side_effects=True, vmem_limit_bytes=VMEM_LIMIT
        ),
        name="samples",
    )(schur, sketch, block_map)


def coupled(schur, basis, block_map, owner_slot):
    dma = pltpu.SemaphoreType.DMA
    return pl.pallas_call(
        coupling_kernel,
        out_shape=(
            jax.ShapeDtypeStruct((2, 1, 256, 256), F32),
            jax.ShapeDtypeStruct((2, 1, 64, 256), F32),
        ),
        in_specs=[pl.BlockSpec(memory_space=pl.ANY), in_vmem(), in_smem(), in_smem()],
        out_specs=(in_vmem(), in_vmem()),
        scratch_shapes=[
            pltpu.VMEM((8, 1024, 256), BF16),
            pltpu.VMEM((8, 128, 256), BF16),
            pltpu.VMEM((8, 256, 256), BF16),
            pltpu.VMEM((2, 4, 256, 256), BF16),
            pltpu.VMEM((4, 256, 256), BF16),
            pltpu.VMEM((1024, 256), F32),
            pltpu.VMEM((4, 256, 256), F32),
            pltpu.VMEM((3, 4, 64, 256), BF16),
            pltpu.VMEM((3, 4, 64, 256), BF16),
            pltpu.VMEM((8, 32, 256), BF16),
            pltpu.VMEM((8, 32, 256), BF16),
            pltpu.VMEM((32, 256), BF16),
            pltpu.VMEM((8, 32, 256), BF16),
            dma((8,)),
            dma((7,)), dma((7,)),
            dma((2, 2, 4)), dma((2, 2, 4)),
            dma((8, 2)), dma((2, 4, 2)),
            dma((3,)), dma((3,)),
            dma((3,)), dma((3,)),
            dma((7,)), dma((7,)),
            dma((7,)), dma((7,)),
        ],
        compiler_params=pltpu.CompilerParams(
            collective_id=1, has_side_effects=True, vmem_limit_bytes=VMEM_LIMIT
        ),
        name="coupling",
    )(schur, basis, block_map, owner_slot)


def shards(schur_blocks, sketch_cols, block_map, owner_slot):
    own, gram = sampled(schur_blocks, sketch_cols, block_map)
    basis = orthonormal(own, gram)
    return coupled(schur_blocks, basis, block_map, owner_slot)


def solution(mesh):
    placed = (P("child", "row", "col"), P("row", None), P(), P())
    return jax.shard_map(
        shards,
        mesh=mesh,
        in_specs=placed,
        out_specs=(P("child", "row", "col", None), P("child", "row", "col", None)),
        check_vma=False,
    )
```

```python
import functools

import jax
import jax.numpy as jnp
from jax import lax
from jax.experimental import pallas as pl
from jax.experimental.pallas import tpu as pltpu
from jax.sharding import PartitionSpec as P

MESH = pl.DeviceIdType.MESH
F32, BF16 = jnp.float32, jnp.bfloat16
HIGHEST = lax.Precision.HIGHEST
VMEM_LIMIT = 60 * 1024 * 1024
SHIFT = 64.0


def ring(value, size):
    return lax.rem(value + 2 * size, size)


def dot(left, right, dims=((1,), (0,)), precision=None):
    return lax.dot_general(left, right, (dims, ((), ())), precision=precision, preferred_element_type=F32)


def hello(peers):
    for peer in peers:
        pl.semaphore_signal(pltpu.get_barrier_semaphore(), inc=1, device_id=peer, device_id_type=MESH)


def met(peers):
    pl.semaphore_wait(pltpu.get_barrier_semaphore(), len(peers))


def send(source, target, send_sem, recv_sem, peer):
    copy = pltpu.make_async_remote_copy(
        src_ref=source,
        dst_ref=target,
        send_sem=send_sem,
        recv_sem=recv_sem,
        device_id=peer,
        device_id_type=MESH,
    )
    copy.start()
    return copy


def place():
    return lax.axis_index("child"), lax.axis_index("row"), lax.axis_index("col")


def columns(chunk):
    return pl.ds(pl.multiple_of(chunk * 256, 256), 256)


def lanes(value, column):
    return jnp.broadcast_to(value[:, column : column + 1], (8, 128))


def sublanes(value, row):
    return jnp.broadcast_to(value[row : row + 1, :], (8, 128))


def inverse_factor(rows, marks):
    sub = lax.broadcasted_iota(jnp.int32, (8, 128), 0)
    for i in range(16):
        left = [[lanes(rows[t], 8 * i + p) for p in range(8)] for t in range(i, 16)]
        inner = {(q, p): sublanes(left[0][p], q) for p in range(8) for q in range(p, 8)}
        upper = [sublanes(rows[i], p) for p in range(8)]
        done = [sublanes(marks[i], p) for p in range(8)]
        for p in range(8):
            scale = lax.rsqrt(inner[p, p])
            for q in range(p + 1, 8):
                inner[q, p] = inner[q, p] * scale
            upper[p] = upper[p] * scale
            done[p] = done[p] * scale
            for t in range(1, 16 - i):
                left[t][p] = left[t][p] * scale
            for q in range(p + 1, 8):
                for s in range(q, 8):
                    inner[s, q] = inner[s, q] - inner[s, p] * inner[q, p]
                upper[q] = upper[q] - inner[q, p] * upper[p]
                done[q] = done[q] - inner[q, p] * done[p]
                for t in range(1, 16 - i):
                    left[t][q] = left[t][q] - left[t][p] * inner[q, p]
        for t in range(1, 16 - i):
            for p in range(8):
                if i + 1 < 16:
                    rows[i + t] = rows[i + t] - left[t][p] * upper[p]
                marks[i + t] = marks[i + t] - left[t][p] * done[p]
        value = done[0]
        for p in range(1, 8):
            value = jnp.where(sub == p, done[p], value)
        marks[i] = value
        yield i


def row_blocks(value):
    return [value[8 * t : 8 * t + 8] for t in range(16)]


def identity(scale):
    row = lax.broadcasted_iota(jnp.int32, (128, 128), 0)
    column = lax.broadcasted_iota(jnp.int32, (128, 128), 1)
    return jnp.where(row == column, scale, 0.0)


def sample_kernel(
    schur, sketch, block_map, own_out, gram_out,
    held, turned, part, sums_out, sums_in, power, total, b_out, b_in, c_out, c_in, z_all,
    load_sem, a_send, a_recv, p_send, p_recv, b_send, b_recv, c_send, c_recv, z_send, z_recv,
):
    c, r, k = place()
    pair, core = lax.div(c, 2), lax.rem(c, 2)
    below, above = {"row": ring(r - 1, 8)}, {"row": ring(r + 1, 8)}
    siblings = [{"child": ring(c + i, 8)} for i in range(1, 8)]
    group = [{"col": ring(k + i, 4)} for i in range(1, 4)]
    cross = [{"child": 2 * pair + 1 - core, "col": ring(k + i, 4)} for i in range(1, 4)]
    peers = [below, above] + siblings + group + cross
    hello(peers)
    loads = {}
    for spot, rel in enumerate((4, 5, 3, 6, 2, 7, 1, 0)):
        chunk = ring(r + rel, 8)
        loads[rel] = pltpu.make_async_copy(schur.at[0, :, columns(chunk)], held.at[chunk], load_sem.at[spot])
        loads[rel].start()
    turned[...] = sketch[...].T

    def produce(rel):
        chunk = ring(r + rel, 8)
        loads[rel].wait()
        part[chunk] = dot(turned[...], held[chunk])

    pending = []
    arriving = {}
    lanesets = ((0, 0), (1, 1), (0, 1), (1, 0))

    def pass_on(s, way, u, step):
        hops = 4 - u if way == 0 else 3 + u
        if step >= hops:
            return
        chunk = ring(r - hops + step if way == 0 else r + hops - step, 8)
        value = part[chunk, pl.ds(128 * s + 64 * u, 64)]
        if step:
            arriving[s, way, u, step - 1].wait_recv()
            value = value + sums_in[s, way, u, step - 1].astype(F32)
        sums_out[s, way, u, step] = value.astype(BF16)
        copy = send(
            sums_out.at[s, way, u, step], sums_in.at[s, way, u, step],
            a_send.at[s, way, u, step], a_recv.at[s, way, u, step], below if way == 0 else above,
        )
        arriving[s, way, u, step] = copy
        pending.append(copy)

    produce(4)
    met(peers)
    for s in range(2):
        pass_on(s, 0, 0, 0)
        pass_on(s, 1, 1, 0)
    produce(5)
    for s in range(2):
        pass_on(s, 0, 1, 0)
    produce(3)
    for s in range(2):
        pass_on(s, 1, 0, 0)
    for step, rels in ((1, (6, 2)), (2, (7, 1)), (3, (0,))):
        for rel in rels:
            produce(rel)
        for s in range(2):
            for way, u in lanesets:
                pass_on(s, way, u, step)

    def finish_sum(s):
        for u in range(2):
            value = part[r, pl.ds(128 * s + 64 * u, 64)]
            for way, hops in ((0, 4 - u), (1, 3 + u)):
                arriving[s, way, u, hops - 1].wait_recv()
                value = value + sums_in[s, way, u, hops - 1].astype(F32)
            power[s, r, pl.ds(64 * u, 64)] = value.astype(BF16)

    coming = {}

    def share(s, way, u, step):
        hops = 4 - u if way == 0 else 3 + u
        if step and step <= hops:
            coming[s, way, u, step - 1].wait_recv()
        if step >= hops:
            return
        chunk = ring(r - step if way == 0 else r + step, 8)
        ref = power.at[s, chunk, pl.ds(64 * u, 64)]
        copy = send(
            ref, ref, p_send.at[s, way, u, step], p_recv.at[s, way, u, step], above if way == 0 else below
        )
        coming[s, way, u, step] = copy
        pending.append(copy)

    def multiply(s, chunk):
        return dot(held[chunk], power[s, chunk], ((1,), (1,)))

    for s in range(2):
        finish_sum(s)
        for way, u in lanesets:
            share(s, way, u, 0)
    for s in range(2):
        total[s] = multiply(s, r)
    for step in range(1, 4):
        for s in range(2):
            for way, u in lanesets:
                share(s, way, u, step)
            total[s] += multiply(s, ring(r - step, 8)) + multiply(s, ring(r + step, 8))

    last = ring(r + 4, 8)
    summed, sent = {}, {}
    for s in range(2):
        share(s, 0, 0, 4)
        share(s, 1, 1, 4)
        sent[s] = []
        for i in (2, 1, 3, 0):
            peer = ring(k + i, 4)
            rows = pl.ds(pl.multiple_of(peer * 256, 256), 256)
            value = total[s, rows] + dot(held[last, rows], power[s, last], ((1,), (1,)))
            if i:
                b_out[s, i - 1] = value.astype(BF16)
                copy = send(
                    b_out.at[s, i - 1], b_in.at[s, i - 1], b_send.at[s, i - 1], b_recv.at[s, i - 1], {"col": peer}
                )
                sent[s].append((i, copy))
                pending.append(copy)
            else:
                total[s, rows] = value

    swapped = {}
    for s in range(2):
        value = total[s, pl.ds(pl.multiple_of(k * 256, 256), 256)]
        for i, copy in sent[s]:
            copy.wait_recv()
            value = value + b_in[s, i - 1].astype(F32)
        c_out[s] = value.astype(BF16).reshape(2, 128, 128)
        swapped[s] = []
        for i in (4, 3, 5, 2, 6, 1, 7):
            peer = ring(c + i, 8)
            copy = send(
                c_out.at[s, lax.rem(peer, 2)], c_in.at[s, c], c_send.at[s, i - 1], c_recv.at[s, i - 1], {"child": peer}
            )
            swapped[s].append(copy)
            pending.append(copy)
        c_in[s, c] = c_out[s, core]

    spot = 8 * r + 2 * k + core
    offset = 2 * k + core
    gathered = {}
    for s in range(2):
        for copy in swapped[s]:
            copy.wait_recv()
        value = jnp.zeros((128, 128), F32)
        for child in range(8):
            wanted = lax.shift_right_logical(block_map[child, spot], 3) == 4 * r + pair
            value = value + c_in[s, child].astype(F32) * jnp.where(wanted, 1.0, 0.0)
        own_out[:, pl.ds(128 * s, 128)] = value
        z_all[s, offset] = value.astype(BF16)
        gathered[s] = []
        ref = z_all.at[s, offset]
        for i in (2, 1, 3, 0):
            for other in range(2):
                if i == 0 and other == 0:
                    continue
                slot = 2 * i + other
                copy = send(
                    ref, ref, z_send.at[s, slot], z_recv.at[s, slot],
                    {"child": c if other == 0 else 2 * pair + 1 - core, "col": ring(k + i, 4)},
                )
                gathered[s].append(copy)
                pending.append(copy)
    for copy in gathered[0]:
        copy.wait_recv()
    first = z_all[0].reshape(1024, 128)
    gram_out[0] = dot(first, first, ((0,), (0,)))
    for copy in gathered[1]:
        copy.wait_recv()
    second = z_all[1].reshape(1024, 128)
    gram_out[1] = dot(second, first, ((0,), (0,)))
    gram_out[2] = dot(second, second, ((0,), (0,)))
    for copy in pending:
        copy.wait_send()


def coupling_kernel(
    schur, own, gram, block_map, owner_slot, basis_out, coupling_out,
    held, inverse, corner, front, b_own, e_low, e_high, mine, column_in, row_in, total, sums,
    f_out, f_in, g_out, g_in, h_out, h_in,
    load_sem, e_send, e_recv, z_send, z_recv, y_send, y_recv, r_send, r_recv, f_send, f_recv, g_send, g_recv,
    h_send, h_recv,
):
    c, r, k = place()
    below, above = {"row": ring(r - 1, 8)}, {"row": ring(r + 1, 8)}
    siblings = [{"child": ring(c + i, 8)} for i in range(1, 8)]
    peers = [below, above] + siblings + [{"col": ring(k + i, 4)} for i in range(1, 4)]
    hello(peers)
    loads = []
    for chunk in range(8):
        loads.append(pltpu.make_async_copy(schur.at[0, :, columns(chunk)], held.at[chunk], load_sem.at[chunk]))
        loads[-1].start()
    pending = []
    outgoing = {}
    e_in = (e_low, e_high)

    def spread(s):
        outgoing[s] = []
        for i in (4, 3, 5, 2, 6, 1, 7):
            copy = send(
                b_own.at[s], e_in[s].at[c], e_send.at[s, i - 1], e_recv.at[s, i - 1], {"child": ring(c + i, 8)}
            )
            outgoing[s].append(copy)
            pending.append(copy)
        e_in[s][c] = b_own[s]

    def select(s):
        for copy in outgoing[s]:
            copy.wait_recv()
        for half in range(2):
            near = lax.rem(lax.shift_right_logical(block_map[c, 8 * r + 2 * k + half], 3), 4)
            mine[s, r, pl.ds(128 * half, 128)] = e_in[s][2 * near + half]

    arriving = {}
    forwards = []
    lanesets = ((0, 0), (1, 1), (0, 1), (1, 0))

    def across(s, rel, half):
        chunk = ring(r + rel, 8)
        peer = lax.div(chunk, 2)
        copy = pltpu.make_async_remote_copy(
            src_ref=mine.at[s, chunk, pl.ds(128 * half, 128)],
            dst_ref=column_in.at[s, lax.rem(chunk, 2), k, pl.ds(128 * half, 128)],
            send_sem=y_send.at[s, rel, half],
            recv_sem=y_recv.at[s, lax.rem(chunk, 2), k, half],
            device_id={"col": peer},
            device_id_type=MESH,
        )
        pl.when(peer != k)(copy.start)
        forwards.append((peer, copy))

    def share(s, step):
        for way, half in lanesets:
            hops = 4 - half if way == 0 else 3 + half
            if step > hops:
                continue
            if step:
                arriving[s, way, half, step - 1].wait_recv()
            if step < hops:
                chunk = ring(r - step if way == 0 else r + step, 8)
                ref = mine.at[s, chunk, pl.ds(128 * half, 128)]
                copy = send(
                    ref, ref, z_send.at[s, way, half, step], z_recv.at[s, way, half, step],
                    above if way == 0 else below,
                )
                arriving[s, way, half, step] = copy
                pending.append(copy)
            if step:
                across(s, (8 - step if way == 0 else step) % 8, half)
        if step == 0:
            for half in range(2):
                across(s, 0, half)

    row_copies = []

    def rows_out(s):
        for i in (2, 1, 3):
            copy = send(
                mine.at[s, r], row_in.at[s, k], r_send.at[s, i - 1], r_recv.at[s, i - 1], {"col": ring(k + i, 4)}
            )
            row_copies.append(copy)
            pending.append(copy)
        row_in[s, k] = mine[s, r]

    def write_basis(s):
        for slot in range(2):
            for half in range(2):
                value = jnp.zeros((128, 128), F32)
                for g in range(4):
                    wanted = owner_slot[4 * r + g] == 2 * c + slot
                    value = value + e_in[s][2 * g + half].astype(F32) * jnp.where(wanted, 1.0, 0.0)
                basis_out[slot, 0, pl.ds(128 * half, 128), pl.ds(128 * s, 128)] = value

    def weigh(s):
        total[s] = dot(held[k], mine[s, 2 * k]) + dot(held[4 + k], mine[s, 2 * k + 1])
        for i in (1, 3, 2):
            peer = ring(k + i, 4)
            for odd in range(2):
                for half in range(2):
                    pltpu.make_async_remote_copy(
                        src_ref=mine.at[s, 0, pl.ds(128 * half, 128)],
                        dst_ref=column_in.at[s, odd, peer, pl.ds(128 * half, 128)],
                        send_sem=y_send.at[s, 0, half],
                        recv_sem=y_recv.at[s, odd, peer, half],
                        device_id={"col": peer},
                        device_id_type=MESH,
                    ).wait_recv()
            total[s] += dot(held[peer], column_in[s, 0, peer]) + dot(held[4 + peer], column_in[s, 1, peer])

    def factor(value, part, actions):
        rows, marks = row_blocks(value), row_blocks(identity(1.0))
        for i in inverse_factor(rows, marks):
            if i in actions:
                actions[i]()
        for t in range(16):
            inverse[part, pl.ds(8 * t, 8)] = marks[t]

    factor(gram[0] + identity(SHIFT), 0, {})
    front[...] = dot(own[:, :128], inverse[0], ((1,), (1,)), HIGHEST)
    b_own[0] = front[...].astype(BF16)
    met(peers)
    spread(0)
    corner[...] = dot(gram[1], inverse[0], ((1,), (1,)), HIGHEST)

    def begin():
        select(0)
        share(0, 0)

    factor(
        gram[2] + identity(SHIFT) - dot(corner[...], corner[...], ((1,), (1,)), HIGHEST), 1, {11: begin}
    )
    rest = own[:, 128:] - dot(front[...], corner[...], ((1,), (1,)), HIGHEST)
    b_own[1] = dot(rest, inverse[1], ((1,), (1,)), HIGHEST).astype(BF16)
    spread(1)
    share(0, 1)
    write_basis(0)
    for load in loads:
        load.wait()
    select(1)
    share(1, 0)
    share(0, 2)
    share(1, 1)
    share(0, 3)
    write_basis(1)
    share(1, 2)
    share(0, 4)
    rows_out(0)
    share(1, 3)
    weigh(0)
    share(1, 4)
    rows_out(1)
    weigh(1)
    for copy in row_copies:
        copy.wait_recv()

    sums[...] = jnp.zeros_like(sums)
    for offset in range(8):
        rows = pl.ds(128 * offset, 128)
        value = jnp.concatenate([total[0, rows], total[1, rows]], axis=1)
        high = value.astype(BF16)
        low = (value - high.astype(F32)).astype(BF16)
        spot = pl.ds(128 * (offset % 2), 128)
        left = jnp.concatenate([row_in[0, offset // 2, spot], row_in[1, offset // 2, spot]], axis=1)
        product = dot(left, high, ((0,), (0,))) + dot(left, low, ((0,), (0,)))
        near = lax.rem(lax.shift_right_logical(block_map[c, 8 * r + offset], 3), 4)
        for g in range(4):
            sums[g] += product * jnp.where(near == g, 1.0, 0.0)

    copies = []
    for i in (2, 1, 3):
        peer = ring(k + i, 4)
        rows = pl.ds(pl.multiple_of(peer * 64, 64), 64)
        f_out[i - 1] = sums[:, rows].astype(BF16)
        copies.append(send(f_out.at[i - 1], f_in.at[i - 1], f_send.at[i - 1], f_recv.at[i - 1], {"col": peer}))
    value = sums[:, pl.ds(pl.multiple_of(k * 64, 64), 64)]
    for copy, i in zip(copies, (2, 1, 3)):
        copy.wait_recv()
        value = value + f_in[i - 1].astype(F32)
    pending += copies
    g_out[...] = value.astype(BF16).reshape(8, 32, 256)
    copies = []
    for i in (4, 3, 5, 2, 6, 1, 7):
        peer = ring(c + i, 8)
        copies.append(send(g_out.at[peer], g_in.at[c], g_send.at[i - 1], g_recv.at[i - 1], {"child": peer}))
    g_in[c] = g_out[c]
    for copy in copies:
        copy.wait_recv()
    pending += copies
    h_out[...] = jnp.sum(g_in[...].astype(F32), axis=0).astype(BF16)
    copies = []
    for i in (4, 3, 5, 2, 6, 1, 7):
        copies.append(send(h_out, h_in.at[c], h_send.at[i - 1], h_recv.at[i - 1], {"child": ring(c + i, 8)}))
    h_in[c] = h_out[...]
    for copy in copies:
        copy.wait_recv()
    pending += copies
    for slot in range(2):
        for half in range(2):
            value = jnp.zeros((32, 256), F32)
            for g in range(4):
                wanted = owner_slot[4 * r + g] == 2 * c + slot
                value = value + h_in[2 * g + half].astype(F32) * jnp.where(wanted, 1.0, 0.0)
            coupling_out[slot, 0, pl.ds(32 * half, 32)] = value
    for copy in pending:
        copy.wait_send()
    for peer, copy in forwards:
        pl.when(peer != k)(copy.wait_send)


def in_vmem():
    return pl.BlockSpec(memory_space=pltpu.VMEM)


def in_smem():
    return pl.BlockSpec(memory_space=pltpu.SMEM)


def sampled(schur, sketch, block_map):
    dma = pltpu.SemaphoreType.DMA
    return pl.pallas_call(
        sample_kernel,
        out_shape=(jax.ShapeDtypeStruct((128, 256), F32), jax.ShapeDtypeStruct((3, 128, 128), F32)),
        in_specs=[pl.BlockSpec(memory_space=pl.ANY), in_vmem(), in_smem()],
        out_specs=(in_vmem(), in_vmem()),
        scratch_shapes=[
            pltpu.VMEM((8, 1024, 256), BF16),
            pltpu.VMEM((256, 1024), BF16),
            pltpu.VMEM((8, 256, 256), F32),
            pltpu.VMEM((2, 2, 2, 4, 64, 256), BF16),
            pltpu.VMEM((2, 2, 2, 4, 64, 256), BF16),
            pltpu.VMEM((2, 8, 128, 256), BF16),
            pltpu.VMEM((2, 1024, 128), F32),
            pltpu.VMEM((2, 3, 256, 128), BF16),
            pltpu.VMEM((2, 3, 256, 128), BF16),
            pltpu.VMEM((2, 2, 128, 128), BF16),
            pltpu.VMEM((2, 8, 128, 128), BF16),
            pltpu.VMEM((2, 8, 128, 128), BF16),
            dma((8,)),
            dma((2, 2, 2, 4)), dma((2, 2, 2, 4)),
            dma((2, 2, 2, 4)), dma((2, 2, 2, 4)),
            dma((2, 3)), dma((2, 3)),
            dma((2, 7)), dma((2, 7)),
            dma((2, 8)), dma((2, 8)),
        ],
        compiler_params=pltpu.CompilerParams(
            collective_id=0, has_side_effects=True, vmem_limit_bytes=VMEM_LIMIT
        ),
        name="samples",
    )(schur, sketch, block_map)


def coupled(schur, own, gram, block_map, owner_slot):
    dma = pltpu.SemaphoreType.DMA
    return pl.pallas_call(
        coupling_kernel,
        out_shape=(
            jax.ShapeDtypeStruct((2, 1, 256, 256), F32),
            jax.ShapeDtypeStruct((2, 1, 64, 256), F32),
        ),
        in_specs=[pl.BlockSpec(memory_space=pl.ANY), in_vmem(), in_vmem(), in_smem(), in_smem()],
        out_specs=(in_vmem(), in_vmem()),
        scratch_shapes=[
            pltpu.VMEM((8, 1024, 256), BF16),
            pltpu.VMEM((2, 128, 128), F32),
            pltpu.VMEM((128, 128), F32),
            pltpu.VMEM((128, 128), F32),
            pltpu.VMEM((2, 128, 128), BF16),
            pltpu.VMEM((8, 128, 128), BF16),
            pltpu.VMEM((8, 128, 128), BF16),
            pltpu.VMEM((2, 8, 256, 128), BF16),
            pltpu.VMEM((2, 2, 4, 256, 128), BF16),
            pltpu.VMEM((2, 4, 256, 128), BF16),
            pltpu.VMEM((2, 1024, 128), F32),
            pltpu.VMEM((4, 256, 256), F32),
            pltpu.VMEM((3, 4, 64, 256), BF16),
            pltpu.VMEM((3, 4, 64, 256), BF16),
            pltpu.VMEM((8, 32, 256), BF16),
            pltpu.VMEM((8, 32, 256), BF16),
            pltpu.VMEM((32, 256), BF16),
            pltpu.VMEM((8, 32, 256), BF16),
            dma((8,)),
            dma((2, 7)), dma((2, 7)),
            dma((2, 2, 2, 4)), dma((2, 2, 2, 4)),
            dma((2, 8, 2)), dma((2, 2, 4, 2)),
            dma((2, 3)), dma((2, 3)),
            dma((3,)), dma((3,)),
            dma((7,)), dma((7,)),
            dma((7,)), dma((7,)),
        ],
        compiler_params=pltpu.CompilerParams(
            collective_id=1, has_side_effects=True, vmem_limit_bytes=VMEM_LIMIT
        ),
        name="coupling",
    )(schur, own, gram, block_map, owner_slot)


def shards(schur_blocks, sketch_cols, block_map, owner_slot):
    own, gram = sampled(schur_blocks, sketch_cols, block_map)
    return coupled(schur_blocks, own, gram, block_map, owner_slot)


def solution(mesh):
    placed = (P("child", "row", "col"), P("row", None), P(), P())
    return jax.shard_map(
        shards,
        mesh=mesh,
        in_specs=placed,
        out_specs=(P("child", "row", "col", None), P("child", "row", "col", None)),
        check_vma=False,
    )
```

```python
import functools

import jax
import jax.numpy as jnp
from jax import lax
from jax.experimental import pallas as pl
from jax.experimental.pallas import tpu as pltpu
from jax.sharding import PartitionSpec as P

MESH = pl.DeviceIdType.MESH
F32, BF16 = jnp.float32, jnp.bfloat16
HIGHEST = lax.Precision.HIGHEST
VMEM_LIMIT = 60 * 1024 * 1024
SHIFT = 64.0


def ring(value, size):
    return lax.rem(value + 2 * size, size)


def dot(left, right, dims=((1,), (0,)), precision=None):
    return lax.dot_general(left, right, (dims, ((), ())), precision=precision, preferred_element_type=F32)


def hello(peers):
    for peer in peers:
        pl.semaphore_signal(pltpu.get_barrier_semaphore(), inc=1, device_id=peer, device_id_type=MESH)


def met(peers):
    pl.semaphore_wait(pltpu.get_barrier_semaphore(), len(peers))


def send(source, target, send_sem, recv_sem, peer):
    copy = pltpu.make_async_remote_copy(
        src_ref=source,
        dst_ref=target,
        send_sem=send_sem,
        recv_sem=recv_sem,
        device_id=peer,
        device_id_type=MESH,
    )
    copy.start()
    return copy


def place():
    return lax.axis_index("child"), lax.axis_index("row"), lax.axis_index("col")


def columns(chunk):
    return pl.ds(pl.multiple_of(chunk * 256, 256), 256)


def lanes(value, column):
    return jnp.broadcast_to(value[:, column : column + 1], (8, 128))


def sublanes(value, row):
    return jnp.broadcast_to(value[row : row + 1, :], (8, 128))


def inverse_factor(rows, marks):
    sub = lax.broadcasted_iota(jnp.int32, (8, 128), 0)
    for i in range(16):
        left = [[lanes(rows[t], 8 * i + p) for p in range(8)] for t in range(i, 16)]
        inner = {(q, p): sublanes(left[0][p], q) for p in range(8) for q in range(p, 8)}
        upper = [sublanes(rows[i], p) for p in range(8)]
        done = [sublanes(marks[i], p) for p in range(8)]
        for p in range(8):
            scale = lax.rsqrt(inner[p, p])
            for q in range(p + 1, 8):
                inner[q, p] = inner[q, p] * scale
            upper[p] = upper[p] * scale
            done[p] = done[p] * scale
            for t in range(1, 16 - i):
                left[t][p] = left[t][p] * scale
            for q in range(p + 1, 8):
                for s in range(q, 8):
                    inner[s, q] = inner[s, q] - inner[s, p] * inner[q, p]
                upper[q] = upper[q] - inner[q, p] * upper[p]
                done[q] = done[q] - inner[q, p] * done[p]
                for t in range(1, 16 - i):
                    left[t][q] = left[t][q] - left[t][p] * inner[q, p]
        for t in range(1, 16 - i):
            for p in range(8):
                if i + 1 < 16:
                    rows[i + t] = rows[i + t] - left[t][p] * upper[p]
                marks[i + t] = marks[i + t] - left[t][p] * done[p]
        value = done[0]
        for p in range(1, 8):
            value = jnp.where(sub == p, done[p], value)
        marks[i] = value
        yield i


def row_blocks(value):
    return [value[8 * t : 8 * t + 8] for t in range(16)]


def identity(scale):
    row = lax.broadcasted_iota(jnp.int32, (128, 128), 0)
    column = lax.broadcasted_iota(jnp.int32, (128, 128), 1)
    return jnp.where(row == column, scale, 0.0)


def sample_kernel(
    schur, sketch, block_map, own_out, gram_out,
    held, turned, part, sums_out, sums_in, power, total, b_out, b_in, c_out, c_in, z_all,
    load_sem, a_send, a_recv, p_send, p_recv, b_send, b_recv, c_send, c_recv, z_send, z_recv,
):
    c, r, k = place()
    pair, core = lax.div(c, 2), lax.rem(c, 2)
    below, above = {"row": ring(r - 1, 8)}, {"row": ring(r + 1, 8)}
    siblings = [{"child": ring(c + i, 8)} for i in range(1, 8)]
    group = [{"col": ring(k + i, 4)} for i in range(1, 4)]
    cross = [{"child": 2 * pair + 1 - core, "col": ring(k + i, 4)} for i in range(1, 4)]
    peers = [below, above] + siblings + group + cross
    hello(peers)
    loads = {}
    for spot, rel in enumerate((4, 5, 3, 6, 2, 7, 1, 0)):
        chunk = ring(r + rel, 8)
        loads[rel] = pltpu.make_async_copy(schur.at[0, :, columns(chunk)], held.at[chunk], load_sem.at[spot])
        loads[rel].start()
    turned[...] = sketch[...].T

    def produce(rel):
        chunk = ring(r + rel, 8)
        loads[rel].wait()
        part[chunk] = dot(turned[...], held[chunk])

    pending = []
    arriving = {}
    lanesets = ((0, 0), (1, 1), (0, 1), (1, 0))

    def pass_on(s, way, u, step):
        hops = 4 - u if way == 0 else 3 + u
        if step >= hops:
            return
        chunk = ring(r - hops + step if way == 0 else r + hops - step, 8)
        value = part[chunk, pl.ds(128 * s + 64 * u, 64)]
        if step:
            arriving[s, way, u, step - 1].wait_recv()
            value = value + sums_in[s, way, u, step - 1].astype(F32)
        sums_out[s, way, u, step] = value.astype(BF16)
        copy = send(
            sums_out.at[s, way, u, step], sums_in.at[s, way, u, step],
            a_send.at[s, way, u, step], a_recv.at[s, way, u, step], below if way == 0 else above,
        )
        arriving[s, way, u, step] = copy
        pending.append(copy)

    produce(4)
    met(peers)
    for s in range(2):
        pass_on(s, 0, 0, 0)
        pass_on(s, 1, 1, 0)
    produce(5)
    for s in range(2):
        pass_on(s, 0, 1, 0)
    produce(3)
    for s in range(2):
        pass_on(s, 1, 0, 0)
    for step, rels in ((1, (6, 2)), (2, (7, 1)), (3, (0,))):
        for rel in rels:
            produce(rel)
        for s in range(2):
            for way, u in lanesets:
                pass_on(s, way, u, step)

    def finish_sum(s):
        for u in range(2):
            value = part[r, pl.ds(128 * s + 64 * u, 64)]
            for way, hops in ((0, 4 - u), (1, 3 + u)):
                arriving[s, way, u, hops - 1].wait_recv()
                value = value + sums_in[s, way, u, hops - 1].astype(F32)
            power[s, r, pl.ds(64 * u, 64)] = value.astype(BF16)

    coming = {}

    def share(s, way, u, step):
        hops = 4 - u if way == 0 else 3 + u
        if step and step <= hops:
            coming[s, way, u, step - 1].wait_recv()
        if step >= hops:
            return
        chunk = ring(r - step if way == 0 else r + step, 8)
        ref = power.at[s, chunk, pl.ds(64 * u, 64)]
        copy = send(
            ref, ref, p_send.at[s, way, u, step], p_recv.at[s, way, u, step], above if way == 0 else below
        )
        coming[s, way, u, step] = copy
        pending.append(copy)

    def multiply(s, chunk):
        return dot(held[chunk], power[s, chunk], ((1,), (1,)))

    for s in range(2):
        finish_sum(s)
        for way, u in lanesets:
            share(s, way, u, 0)
    for s in range(2):
        total[s] = multiply(s, r)
    for step in range(1, 4):
        for s in range(2):
            for way, u in lanesets:
                share(s, way, u, step)
            total[s] += multiply(s, ring(r - step, 8)) + multiply(s, ring(r + step, 8))

    last = ring(r + 4, 8)
    summed, sent = {}, {}
    for s in range(2):
        share(s, 0, 0, 4)
        share(s, 1, 1, 4)
        sent[s] = []
        for i in (2, 1, 3, 0):
            peer = ring(k + i, 4)
            rows = pl.ds(pl.multiple_of(peer * 256, 256), 256)
            value = total[s, rows] + dot(held[last, rows], power[s, last], ((1,), (1,)))
            if i:
                b_out[s, i - 1] = value.astype(BF16)
                copy = send(
                    b_out.at[s, i - 1], b_in.at[s, i - 1], b_send.at[s, i - 1], b_recv.at[s, i - 1], {"col": peer}
                )
                sent[s].append((i, copy))
                pending.append(copy)
            else:
                total[s, rows] = value

    swapped = {}
    for s in range(2):
        value = total[s, pl.ds(pl.multiple_of(k * 256, 256), 256)]
        for i, copy in sent[s]:
            copy.wait_recv()
            value = value + b_in[s, i - 1].astype(F32)
        c_out[s] = value.astype(BF16).reshape(2, 128, 128)
        swapped[s] = []
        for i in (4, 3, 5, 2, 6, 1, 7):
            peer = ring(c + i, 8)
            copy = send(
                c_out.at[s, lax.rem(peer, 2)], c_in.at[s, c], c_send.at[s, i - 1], c_recv.at[s, i - 1], {"child": peer}
            )
            swapped[s].append(copy)
            pending.append(copy)
        c_in[s, c] = c_out[s, core]

    spot = 8 * r + 2 * k + core
    offset = 2 * k + core
    gathered = {}
    for s in range(2):
        for copy in swapped[s]:
            copy.wait_recv()
        value = jnp.zeros((128, 128), F32)
        for child in range(8):
            wanted = lax.shift_right_logical(block_map[child, spot], 3) == 4 * r + pair
            value = value + c_in[s, child].astype(F32) * jnp.where(wanted, 1.0, 0.0)
        own_out[:, pl.ds(128 * s, 128)] = value
        z_all[s, offset] = value.astype(BF16)
        gathered[s] = []
        ref = z_all.at[s, offset]
        for i in (2, 1, 3, 0):
            for other in range(2):
                if i == 0 and other == 0:
                    continue
                slot = 2 * i + other
                copy = send(
                    ref, ref, z_send.at[s, slot], z_recv.at[s, slot],
                    {"child": c if other == 0 else 2 * pair + 1 - core, "col": ring(k + i, 4)},
                )
                gathered[s].append(copy)
                pending.append(copy)
    for copy in gathered[0]:
        copy.wait_recv()
    first = z_all[0].reshape(1024, 128)
    gram_out[0] = dot(first, first, ((0,), (0,)))
    for copy in gathered[1]:
        copy.wait_recv()
    second = z_all[1].reshape(1024, 128)
    gram_out[1] = dot(second, first, ((0,), (0,)))
    gram_out[2] = dot(second, second, ((0,), (0,)))
    for copy in pending:
        copy.wait_send()


def coupling_kernel(
    schur, own, gram, block_map, basis_out, coupling_out,
    held, inverse, corner, front, b_own, e_low, e_high, mine, column_in, row_in, total, sums,
    f_out, f_in, x_out, x_in, g_out, g_in, v_sum, v_out, v_in, h_out, h_in,
    load_sem, e_send, e_recv, z_send, z_recv, y_send, y_recv, r_send, r_recv, f_send, f_recv, x_send, x_recv,
    g_send, g_recv, v_send, v_recv, h_send, h_recv,
):
    c, r, k = place()
    below, above = {"row": ring(r - 1, 8)}, {"row": ring(r + 1, 8)}
    siblings = [{"child": ring(c + i, 8)} for i in range(1, 8)]
    peers = [below, above] + siblings + [{"col": ring(k + i, 4)} for i in range(1, 4)]
    hello(peers)
    loads = []
    for chunk in range(8):
        loads.append(pltpu.make_async_copy(schur.at[0, :, columns(chunk)], held.at[chunk], load_sem.at[chunk]))
        loads[-1].start()
    pending = []
    outgoing = {}
    e_in = (e_low, e_high)

    def spread(s):
        outgoing[s] = []
        for i in (4, 3, 5, 2, 6, 1, 7):
            copy = send(
                b_own.at[s], e_in[s].at[c], e_send.at[s, i - 1], e_recv.at[s, i - 1], {"child": ring(c + i, 8)}
            )
            outgoing[s].append(copy)
            pending.append(copy)
        e_in[s][c] = b_own[s]

    def select(s):
        for copy in outgoing[s]:
            copy.wait_recv()
        for half in range(2):
            near = lax.rem(lax.shift_right_logical(block_map[c, 8 * r + 2 * k + half], 3), 4)
            mine[s, r, pl.ds(128 * half, 128)] = e_in[s][2 * near + half]

    arriving = {}
    forwards = []
    lanesets = ((0, 0), (1, 1), (0, 1), (1, 0))

    def across(s, rel, half):
        chunk = ring(r + rel, 8)
        peer = lax.div(chunk, 2)
        copy = pltpu.make_async_remote_copy(
            src_ref=mine.at[s, chunk, pl.ds(128 * half, 128)],
            dst_ref=column_in.at[s, lax.rem(chunk, 2), k, pl.ds(128 * half, 128)],
            send_sem=y_send.at[s, rel, half],
            recv_sem=y_recv.at[s, lax.rem(chunk, 2), k, half],
            device_id={"col": peer},
            device_id_type=MESH,
        )
        pl.when(peer != k)(copy.start)
        forwards.append((peer, copy))

    def share(s, step):
        for way, half in lanesets:
            hops = 4 - half if way == 0 else 3 + half
            if step > hops:
                continue
            if step:
                arriving[s, way, half, step - 1].wait_recv()
            if step < hops:
                chunk = ring(r - step if way == 0 else r + step, 8)
                ref = mine.at[s, chunk, pl.ds(128 * half, 128)]
                copy = send(
                    ref, ref, z_send.at[s, way, half, step], z_recv.at[s, way, half, step],
                    above if way == 0 else below,
                )
                arriving[s, way, half, step] = copy
                pending.append(copy)
            if step:
                across(s, (8 - step if way == 0 else step) % 8, half)
        if step == 0:
            for half in range(2):
                across(s, 0, half)

    row_copies = []

    def rows_out(s):
        for i in (2, 1, 3):
            copy = send(
                mine.at[s, r], row_in.at[s, k], r_send.at[s, i - 1], r_recv.at[s, i - 1], {"col": ring(k + i, 4)}
            )
            row_copies.append(copy)
            pending.append(copy)
        row_in[s, k] = mine[s, r]

    def write_basis(s):
        basis_out[s] = e_in[s][...]

    def weigh(s):
        total[s] = dot(held[k], mine[s, 2 * k]) + dot(held[4 + k], mine[s, 2 * k + 1])
        for i in (1, 3, 2):
            peer = ring(k + i, 4)
            for odd in range(2):
                for half in range(2):
                    pltpu.make_async_remote_copy(
                        src_ref=mine.at[s, 0, pl.ds(128 * half, 128)],
                        dst_ref=column_in.at[s, odd, peer, pl.ds(128 * half, 128)],
                        send_sem=y_send.at[s, 0, half],
                        recv_sem=y_recv.at[s, odd, peer, half],
                        device_id={"col": peer},
                        device_id_type=MESH,
                    ).wait_recv()
            total[s] += dot(held[peer], column_in[s, 0, peer]) + dot(held[4 + peer], column_in[s, 1, peer])

    def factor(value, part, actions):
        rows, marks = row_blocks(value), row_blocks(identity(1.0))
        for i in inverse_factor(rows, marks):
            if i in actions:
                actions[i]()
        for t in range(16):
            inverse[part, pl.ds(8 * t, 8)] = marks[t]

    factor(gram[0] + identity(SHIFT), 0, {})
    front[...] = dot(own[:, :128], inverse[0], ((1,), (1,)), HIGHEST)
    b_own[0] = front[...].astype(BF16)
    met(peers)
    spread(0)
    corner[...] = dot(gram[1], inverse[0], ((1,), (1,)), HIGHEST)

    def begin():
        select(0)
        share(0, 0)

    factor(
        gram[2] + identity(SHIFT) - dot(corner[...], corner[...], ((1,), (1,)), HIGHEST), 1, {11: begin}
    )
    rest = own[:, 128:] - dot(front[...], corner[...], ((1,), (1,)), HIGHEST)
    b_own[1] = dot(rest, inverse[1], ((1,), (1,)), HIGHEST).astype(BF16)
    spread(1)
    share(0, 1)
    write_basis(0)
    for load in loads:
        load.wait()
    select(1)
    share(1, 0)
    share(0, 2)
    share(1, 1)
    share(0, 3)
    write_basis(1)
    share(1, 2)
    share(0, 4)
    rows_out(0)
    share(1, 3)
    weigh(0)
    share(1, 4)
    rows_out(1)
    weigh(1)
    for copy in row_copies:
        copy.wait_recv()

    sums[...] = jnp.zeros_like(sums)
    for offset in range(8):
        rows = pl.ds(128 * offset, 128)
        value = jnp.concatenate([total[0, rows], total[1, rows]], axis=1)
        high = value.astype(BF16)
        low = (value - high.astype(F32)).astype(BF16)
        spot = pl.ds(128 * (offset % 2), 128)
        left = jnp.concatenate([row_in[0, offset // 2, spot], row_in[1, offset // 2, spot]], axis=1)
        product = dot(left, high, ((0,), (0,))) + dot(left, low, ((0,), (0,)))
        near = lax.rem(lax.shift_right_logical(block_map[c, 8 * r + offset], 3), 4)
        for g in range(4):
            sums[g] += product * jnp.where(near == g, 1.0, 0.0)

    for g in range(2):
        quarters = sums[2 + g].astype(BF16).reshape(4, 4, 16, 256)
        for q in range(4):
            x_out[4 * g + q] = quarters[:, q]
    x_copies, copies = [], []
    for i in (2, 1, 3):
        peer = ring(k + i, 4)
        rows = pl.ds(pl.multiple_of(peer * 64, 64), 64)
        f_out[i - 1] = sums[:2, rows].astype(BF16)
        copies.append(send(f_out.at[i - 1], f_in.at[i - 1], f_send.at[i - 1], f_recv.at[i - 1], {"col": peer}))
    for i in (4, 3, 5, 2, 6, 1, 7):
        peer = ring(c + i, 8)
        x_copies.append(send(x_out.at[peer], x_in.at[c], x_send.at[i - 1], x_recv.at[i - 1], {"child": peer}))
    x_in[c] = x_out[c]
    value = sums[:2, pl.ds(pl.multiple_of(k * 64, 64), 64)]
    for copy, i in zip(copies, (2, 1, 3)):
        copy.wait_recv()
        value = value + f_in[i - 1].astype(F32)
    pending += copies
    g_out[...] = value.astype(BF16).reshape(8, 16, 256)
    g_copies = []
    for i in (4, 3, 5, 2, 6, 1, 7):
        peer = ring(c + i, 8)
        g_copies.append(send(g_out.at[peer], g_in.at[c], g_send.at[i - 1], g_recv.at[i - 1], {"child": peer}))
    g_in[c] = g_out[c]
    for copy in x_copies:
        copy.wait_recv()
    pending += x_copies
    v_sum[...] = jnp.sum(x_in[...].astype(F32), axis=0)
    v_out[...] = v_sum[...].astype(BF16)
    copies = []
    for i in (2, 1, 3):
        peer = ring(k + i, 4)
        copies.append(send(v_out.at[peer], v_in.at[i - 1], v_send.at[i - 1], v_recv.at[i - 1], {"col": peer}))
    for copy in g_copies:
        copy.wait_recv()
    pending += g_copies
    h_out[0] = jnp.sum(g_in[...].astype(F32), axis=0).astype(BF16)
    value = v_sum[k]
    for copy, i in zip(copies, (2, 1, 3)):
        copy.wait_recv()
        value = value + v_in[i - 1].astype(F32)
    pending += copies
    h_out[1] = value.astype(BF16)
    copies = []
    for i in (4, 3, 5, 2, 6, 1, 7):
        copies.append(send(h_out, h_in.at[c], h_send.at[i - 1], h_recv.at[i - 1], {"child": ring(c + i, 8)}))
    h_in[c] = h_out[...]
    for copy in copies:
        copy.wait_recv()
    pending += copies
    coupling_out[...] = h_in[...]
    for copy in pending:
        copy.wait_send()
    for peer, copy in forwards:
        pl.when(peer != k)(copy.wait_send)


def in_vmem():
    return pl.BlockSpec(memory_space=pltpu.VMEM)


def in_smem():
    return pl.BlockSpec(memory_space=pltpu.SMEM)


def sampled(schur, sketch, block_map):
    dma = pltpu.SemaphoreType.DMA
    return pl.pallas_call(
        sample_kernel,
        out_shape=(jax.ShapeDtypeStruct((128, 256), F32), jax.ShapeDtypeStruct((3, 128, 128), F32)),
        in_specs=[pl.BlockSpec(memory_space=pl.ANY), in_vmem(), in_smem()],
        out_specs=(in_vmem(), in_vmem()),
        scratch_shapes=[
            pltpu.VMEM((8, 1024, 256), BF16),
            pltpu.VMEM((256, 1024), BF16),
            pltpu.VMEM((8, 256, 256), F32),
            pltpu.VMEM((2, 2, 2, 4, 64, 256), BF16),
            pltpu.VMEM((2, 2, 2, 4, 64, 256), BF16),
            pltpu.VMEM((2, 8, 128, 256), BF16),
            pltpu.VMEM((2, 1024, 128), F32),
            pltpu.VMEM((2, 3, 256, 128), BF16),
            pltpu.VMEM((2, 3, 256, 128), BF16),
            pltpu.VMEM((2, 2, 128, 128), BF16),
            pltpu.VMEM((2, 8, 128, 128), BF16),
            pltpu.VMEM((2, 8, 128, 128), BF16),
            dma((8,)),
            dma((2, 2, 2, 4)), dma((2, 2, 2, 4)),
            dma((2, 2, 2, 4)), dma((2, 2, 2, 4)),
            dma((2, 3)), dma((2, 3)),
            dma((2, 7)), dma((2, 7)),
            dma((2, 8)), dma((2, 8)),
        ],
        compiler_params=pltpu.CompilerParams(
            collective_id=0, has_side_effects=True, vmem_limit_bytes=VMEM_LIMIT
        ),
        name="samples",
    )(schur, sketch, block_map)


def coupled(schur, own, gram, block_map):
    dma = pltpu.SemaphoreType.DMA
    return pl.pallas_call(
        coupling_kernel,
        out_shape=(
            jax.ShapeDtypeStruct((2, 8, 128, 128), BF16),
            jax.ShapeDtypeStruct((8, 2, 16, 256), BF16),
        ),
        in_specs=[pl.BlockSpec(memory_space=pl.ANY), in_vmem(), in_vmem(), in_smem()],
        out_specs=(in_vmem(), in_vmem()),
        scratch_shapes=[
            pltpu.VMEM((8, 1024, 256), BF16),
            pltpu.VMEM((2, 128, 128), F32),
            pltpu.VMEM((128, 128), F32),
            pltpu.VMEM((128, 128), F32),
            pltpu.VMEM((2, 128, 128), BF16),
            pltpu.VMEM((8, 128, 128), BF16),
            pltpu.VMEM((8, 128, 128), BF16),
            pltpu.VMEM((2, 8, 256, 128), BF16),
            pltpu.VMEM((2, 2, 4, 256, 128), BF16),
            pltpu.VMEM((2, 4, 256, 128), BF16),
            pltpu.VMEM((2, 1024, 128), F32),
            pltpu.VMEM((4, 256, 256), F32),
            pltpu.VMEM((3, 2, 64, 256), BF16),
            pltpu.VMEM((3, 2, 64, 256), BF16),
            pltpu.VMEM((8, 4, 16, 256), BF16),
            pltpu.VMEM((8, 4, 16, 256), BF16),
            pltpu.VMEM((8, 16, 256), BF16),
            pltpu.VMEM((8, 16, 256), BF16),
            pltpu.VMEM((4, 16, 256), F32),
            pltpu.VMEM((4, 16, 256), BF16),
            pltpu.VMEM((3, 16, 256), BF16),
            pltpu.VMEM((2, 16, 256), BF16),
            pltpu.VMEM((8, 2, 16, 256), BF16),
            dma((8,)),
            dma((2, 7)), dma((2, 7)),
            dma((2, 2, 2, 4)), dma((2, 2, 2, 4)),
            dma((2, 8, 2)), dma((2, 2, 4, 2)),
            dma((2, 3)), dma((2, 3)),
            dma((3,)), dma((3,)),
            dma((7,)), dma((7,)),
            dma((7,)), dma((7,)),
            dma((3,)), dma((3,)),
            dma((7,)), dma((7,)),
        ],
        compiler_params=pltpu.CompilerParams(
            collective_id=1, has_side_effects=True, vmem_limit_bytes=VMEM_LIMIT
        ),
        name="coupling",
    )(schur, own, gram, block_map)


def place_kernel(basis, coupling, owner_slot, basis_out, coupling_out):
    c, r = lax.axis_index("child"), lax.axis_index("row")
    for slot in range(2):
        share = [jnp.where(owner_slot[4 * r + g] == 2 * c + slot, 1.0, 0.0) for g in range(4)]
        for half in range(2):
            for s in range(2):
                value = basis[s, half].astype(F32) * share[0]
                for g in range(1, 4):
                    value = value + basis[s, 2 * g + half].astype(F32) * share[g]
                basis_out[slot, 0, pl.ds(128 * half, 128), pl.ds(128 * s, 128)] = value
        for q in range(4):
            value = coupling[q, 0].astype(F32) * share[0]
            for g in range(1, 4):
                value = value + coupling[4 * (g % 2) + q, g // 2].astype(F32) * share[g]
            coupling_out[slot, 0, pl.ds(16 * q, 16)] = value


def placed_results(basis, coupling, owner_slot):
    return pl.pallas_call(
        place_kernel,
        out_shape=(
            jax.ShapeDtypeStruct((2, 1, 256, 256), F32),
            jax.ShapeDtypeStruct((2, 1, 64, 256), F32),
        ),
        in_specs=[in_vmem(), in_vmem(), in_smem()],
        out_specs=(in_vmem(), in_vmem()),
        name="results",
    )(basis, coupling, owner_slot)


def shards(schur_blocks, sketch_cols, block_map, owner_slot):
    own, gram = sampled(schur_blocks, sketch_cols, block_map)
    basis, coupling = coupled(schur_blocks, own, gram, block_map)
    return placed_results(basis, coupling, owner_slot)


def solution(mesh):
    placed = (P("child", "row", "col"), P("row", None), P(), P())
    return jax.shard_map(
        shards,
        mesh=mesh,
        in_specs=placed,
        out_specs=(P("child", "row", "col", None), P("child", "row", "col", None)),
        check_vma=False,
    )
```

```python
import functools

import jax
import jax.numpy as jnp
from jax import lax
from jax.experimental import pallas as pl
from jax.experimental.pallas import tpu as pltpu
from jax.sharding import PartitionSpec as P

MESH = pl.DeviceIdType.MESH
F32, BF16 = jnp.float32, jnp.bfloat16
HIGHEST = lax.Precision.HIGHEST
VMEM_LIMIT = 60 * 1024 * 1024
SHIFT = 64.0


def ring(value, size):
    return lax.rem(value + 2 * size, size)


def dot(left, right, dims=((1,), (0,)), precision=None):
    return lax.dot_general(left, right, (dims, ((), ())), precision=precision, preferred_element_type=F32)


def hello(peers):
    for peer in peers:
        pl.semaphore_signal(pltpu.get_barrier_semaphore(), inc=1, device_id=peer, device_id_type=MESH)


def met(peers):
    pl.semaphore_wait(pltpu.get_barrier_semaphore(), len(peers))


def send(source, target, send_sem, recv_sem, peer):
    copy = pltpu.make_async_remote_copy(
        src_ref=source,
        dst_ref=target,
        send_sem=send_sem,
        recv_sem=recv_sem,
        device_id=peer,
        device_id_type=MESH,
    )
    copy.start()
    return copy


def place():
    return lax.axis_index("child"), lax.axis_index("row"), lax.axis_index("col")


def columns(chunk):
    return pl.ds(pl.multiple_of(chunk * 256, 256), 256)


def lanes(value, column):
    return jnp.broadcast_to(value[:, column : column + 1], (8, 128))


def sublanes(value, row):
    return jnp.broadcast_to(value[row : row + 1, :], (8, 128))


def inverse_factor(rows, marks):
    sub = lax.broadcasted_iota(jnp.int32, (8, 128), 0)
    for i in range(16):
        left = [[lanes(rows[t], 8 * i + p) for p in range(8)] for t in range(i, 16)]
        inner = {(q, p): sublanes(left[0][p], q) for p in range(8) for q in range(p, 8)}
        upper = [sublanes(rows[i], p) for p in range(8)]
        done = [sublanes(marks[i], p) for p in range(8)]
        for p in range(8):
            scale = lax.rsqrt(inner[p, p])
            for q in range(p + 1, 8):
                inner[q, p] = inner[q, p] * scale
            upper[p] = upper[p] * scale
            done[p] = done[p] * scale
            for t in range(1, 16 - i):
                left[t][p] = left[t][p] * scale
            for q in range(p + 1, 8):
                for s in range(q, 8):
                    inner[s, q] = inner[s, q] - inner[s, p] * inner[q, p]
                upper[q] = upper[q] - inner[q, p] * upper[p]
                done[q] = done[q] - inner[q, p] * done[p]
                for t in range(1, 16 - i):
                    left[t][q] = left[t][q] - left[t][p] * inner[q, p]
        for t in range(1, 16 - i):
            for p in range(8):
                if i + 1 < 16:
                    rows[i + t] = rows[i + t] - left[t][p] * upper[p]
                marks[i + t] = marks[i + t] - left[t][p] * done[p]
        value = done[0]
        for p in range(1, 8):
            value = jnp.where(sub == p, done[p], value)
        marks[i] = value
        yield i


def row_blocks(value):
    return [value[8 * t : 8 * t + 8] for t in range(16)]


def identity(scale):
    row = lax.broadcasted_iota(jnp.int32, (128, 128), 0)
    column = lax.broadcasted_iota(jnp.int32, (128, 128), 1)
    return jnp.where(row == column, scale, 0.0)


def sample_kernel(
    schur, sketch, block_map, own_out, gram_out,
    held, turned, part, sums_out, sums_in, power, total, b_out, b_in, c_out, c_in, z_all,
    load_sem, a_send, a_recv, p_send, p_recv, b_send, b_recv, c_send, c_recv, z_send, z_recv,
):
    c, r, k = place()
    pair, core = lax.div(c, 2), lax.rem(c, 2)
    below, above = {"row": ring(r - 1, 8)}, {"row": ring(r + 1, 8)}
    siblings = [{"child": ring(c + i, 8)} for i in range(1, 8)]
    group = [{"col": ring(k + i, 4)} for i in range(1, 4)]
    cross = [{"child": 2 * pair + 1 - core, "col": ring(k + i, 4)} for i in range(1, 4)]
    peers = [below, above] + siblings + group + cross
    hello(peers)
    loads = {}
    for spot, rel in enumerate((4, 5, 3, 6, 2, 7, 1, 0)):
        chunk = ring(r + rel, 8)
        loads[rel] = pltpu.make_async_copy(schur.at[0, :, columns(chunk)], held.at[chunk], load_sem.at[spot])
        loads[rel].start()
    turned[...] = sketch[...].T

    def produce(rel):
        chunk = ring(r + rel, 8)
        loads[rel].wait()
        part[chunk] = dot(turned[...], held[chunk])

    pending = []
    arriving = {}
    lanesets = ((0, 0), (1, 1), (0, 1), (1, 0))

    def pass_on(s, way, u, step):
        hops = 4 - u if way == 0 else 3 + u
        if step >= hops:
            return
        chunk = ring(r - hops + step if way == 0 else r + hops - step, 8)
        value = part[chunk, pl.ds(128 * s + 64 * u, 64)]
        if step:
            arriving[s, way, u, step - 1].wait_recv()
            value = value + sums_in[s, way, u, step - 1].astype(F32)
        sums_out[s, way, u, step] = value.astype(BF16)
        copy = send(
            sums_out.at[s, way, u, step], sums_in.at[s, way, u, step],
            a_send.at[s, way, u, step], a_recv.at[s, way, u, step], below if way == 0 else above,
        )
        arriving[s, way, u, step] = copy
        pending.append(copy)

    produce(4)
    met(peers)
    for s in range(2):
        pass_on(s, 0, 0, 0)
        pass_on(s, 1, 1, 0)
    produce(5)
    for s in range(2):
        pass_on(s, 0, 1, 0)
    produce(3)
    for s in range(2):
        pass_on(s, 1, 0, 0)
    for step, rels in ((1, (6, 2)), (2, (7, 1)), (3, (0,))):
        for rel in rels:
            produce(rel)
        for s in range(2):
            for way, u in lanesets:
                pass_on(s, way, u, step)

    def finish_sum(s):
        for u in range(2):
            value = part[r, pl.ds(128 * s + 64 * u, 64)]
            for way, hops in ((0, 4 - u), (1, 3 + u)):
                arriving[s, way, u, hops - 1].wait_recv()
                value = value + sums_in[s, way, u, hops - 1].astype(F32)
            power[s, r, pl.ds(64 * u, 64)] = value.astype(BF16)

    coming = {}

    def share(s, way, u, step):
        hops = 4 - u if way == 0 else 3 + u
        if step and step <= hops:
            coming[s, way, u, step - 1].wait_recv()
        if step >= hops:
            return
        chunk = ring(r - step if way == 0 else r + step, 8)
        ref = power.at[s, chunk, pl.ds(64 * u, 64)]
        copy = send(
            ref, ref, p_send.at[s, way, u, step], p_recv.at[s, way, u, step], above if way == 0 else below
        )
        coming[s, way, u, step] = copy
        pending.append(copy)

    def multiply(s, chunk):
        return dot(held[chunk], power[s, chunk], ((1,), (1,)))

    for s in range(2):
        finish_sum(s)
        for way, u in lanesets:
            share(s, way, u, 0)
    for s in range(2):
        total[s] = multiply(s, r)
    for step in range(1, 4):
        for s in range(2):
            for way, u in lanesets:
                share(s, way, u, step)
            total[s] += multiply(s, ring(r - step, 8)) + multiply(s, ring(r + step, 8))

    last = ring(r + 4, 8)
    summed, sent = {}, {}
    for s in range(2):
        share(s, 0, 0, 4)
        share(s, 1, 1, 4)
        sent[s] = []
        for i in (2, 1, 3, 0):
            peer = ring(k + i, 4)
            rows = pl.ds(pl.multiple_of(peer * 256, 256), 256)
            value = total[s, rows] + dot(held[last, rows], power[s, last], ((1,), (1,)))
            if i:
                b_out[s, i - 1] = value.astype(BF16)
                copy = send(
                    b_out.at[s, i - 1], b_in.at[s, i - 1], b_send.at[s, i - 1], b_recv.at[s, i - 1], {"col": peer}
                )
                sent[s].append((i, copy))
                pending.append(copy)
            else:
                total[s, rows] = value

    swapped = {}
    for s in range(2):
        value = total[s, pl.ds(pl.multiple_of(k * 256, 256), 256)]
        for i, copy in sent[s]:
            copy.wait_recv()
            value = value + b_in[s, i - 1].astype(F32)
        c_out[s] = value.astype(BF16).reshape(2, 128, 128)
        swapped[s] = []
        for i in (4, 3, 5, 2, 6, 1, 7):
            peer = ring(c + i, 8)
            copy = send(
                c_out.at[s, lax.rem(peer, 2)], c_in.at[s, c], c_send.at[s, i - 1], c_recv.at[s, i - 1], {"child": peer}
            )
            swapped[s].append(copy)
            pending.append(copy)
        c_in[s, c] = c_out[s, core]

    spot = 8 * r + 2 * k + core
    offset = 2 * k + core
    gathered = {}
    for s in range(2):
        for copy in swapped[s]:
            copy.wait_recv()
        value = jnp.zeros((128, 128), F32)
        for child in range(8):
            wanted = lax.shift_right_logical(block_map[child, spot], 3) == 4 * r + pair
            value = value + c_in[s, child].astype(F32) * jnp.where(wanted, 1.0, 0.0)
        own_out[:, pl.ds(128 * s, 128)] = value
        z_all[s, offset] = value.astype(BF16)
        gathered[s] = []
        ref = z_all.at[s, offset]
        for i in (2, 1, 3, 0):
            for other in range(2):
                if i == 0 and other == 0:
                    continue
                slot = 2 * i + other
                copy = send(
                    ref, ref, z_send.at[s, slot], z_recv.at[s, slot],
                    {"child": c if other == 0 else 2 * pair + 1 - core, "col": ring(k + i, 4)},
                )
                gathered[s].append(copy)
                pending.append(copy)
    for copy in gathered[0]:
        copy.wait_recv()
    first = z_all[0].reshape(1024, 128)
    gram_out[0] = dot(first, first, ((0,), (0,)))
    for copy in gathered[1]:
        copy.wait_recv()
    second = z_all[1].reshape(1024, 128)
    gram_out[1] = dot(second, first, ((0,), (0,)))
    gram_out[2] = dot(second, second, ((0,), (0,)))
    for copy in pending:
        copy.wait_send()


def coupling_kernel(
    schur, own, gram, block_map, basis_out, coupling_out,
    held, inverse, corner, front, b_own, e_low, e_high, mine, column_in, row_in, total, sums,
    f_out, f_in, x_out, x_in, g_out, g_in, v_sum, v_out, v_in, h_out, h_in,
    load_sem, e_send, e_recv, z_send, z_recv, y_send, y_recv, r_send, r_recv, f_send, f_recv, x_send, x_recv,
    g_send, g_recv, v_send, v_recv, h_send, h_recv,
):
    c, r, k = place()
    below, above = {"row": ring(r - 1, 8)}, {"row": ring(r + 1, 8)}
    siblings = [{"child": ring(c + i, 8)} for i in range(1, 8)]
    peers = [below, above] + siblings + [{"col": ring(k + i, 4)} for i in range(1, 4)]
    hello(peers)
    loads = []
    for chunk in range(8):
        loads.append(pltpu.make_async_copy(schur.at[0, :, columns(chunk)], held.at[chunk], load_sem.at[chunk]))
        loads[-1].start()
    pending = []
    outgoing = {}
    e_in = (e_low, e_high)

    def spread(s):
        outgoing[s] = []
        for i in (4, 3, 5, 2, 6, 1, 7):
            copy = send(
                b_own.at[s], e_in[s].at[c], e_send.at[s, i - 1], e_recv.at[s, i - 1], {"child": ring(c + i, 8)}
            )
            outgoing[s].append(copy)
            pending.append(copy)
        e_in[s][c] = b_own[s]

    def select(s):
        for copy in outgoing[s]:
            copy.wait_recv()
        for half in range(2):
            near = lax.rem(lax.shift_right_logical(block_map[c, 8 * r + 2 * k + half], 3), 4)
            mine[s, r, pl.ds(128 * half, 128)] = e_in[s][2 * near + half]

    arriving = {}
    forwards = []
    lanesets = ((0, 0), (1, 1), (0, 1), (1, 0))

    def across(s, rel, half):
        chunk = ring(r + rel, 8)
        peer = lax.div(chunk, 2)
        copy = pltpu.make_async_remote_copy(
            src_ref=mine.at[s, chunk, pl.ds(128 * half, 128)],
            dst_ref=column_in.at[s, lax.rem(chunk, 2), k, pl.ds(128 * half, 128)],
            send_sem=y_send.at[s, rel, half],
            recv_sem=y_recv.at[s, lax.rem(chunk, 2), k, half],
            device_id={"col": peer},
            device_id_type=MESH,
        )
        pl.when(peer != k)(copy.start)
        forwards.append((peer, copy))

    def share(s, step):
        for way, half in lanesets:
            hops = 4 - half if way == 0 else 3 + half
            if step > hops:
                continue
            if step:
                arriving[s, way, half, step - 1].wait_recv()
            if step < hops:
                chunk = ring(r - step if way == 0 else r + step, 8)
                ref = mine.at[s, chunk, pl.ds(128 * half, 128)]
                copy = send(
                    ref, ref, z_send.at[s, way, half, step], z_recv.at[s, way, half, step],
                    above if way == 0 else below,
                )
                arriving[s, way, half, step] = copy
                pending.append(copy)
            if step:
                across(s, (8 - step if way == 0 else step) % 8, half)
        if step == 0:
            for half in range(2):
                across(s, 0, half)

    row_copies = []

    def rows_out(s):
        for i in (2, 1, 3):
            copy = send(
                mine.at[s, r], row_in.at[s, k], r_send.at[s, i - 1], r_recv.at[s, i - 1], {"col": ring(k + i, 4)}
            )
            row_copies.append(copy)
            pending.append(copy)
        row_in[s, k] = mine[s, r]

    def write_basis(s):
        basis_out[s] = e_in[s][...]

    def weigh_own(s):
        total[s] = dot(held[k], mine[s, 2 * k]) + dot(held[4 + k], mine[s, 2 * k + 1])

    def weigh(s):
        for i in (1, 3, 2):
            peer = ring(k + i, 4)
            for odd in range(2):
                for half in range(2):
                    pltpu.make_async_remote_copy(
                        src_ref=mine.at[s, 0, pl.ds(128 * half, 128)],
                        dst_ref=column_in.at[s, odd, peer, pl.ds(128 * half, 128)],
                        send_sem=y_send.at[s, 0, half],
                        recv_sem=y_recv.at[s, odd, peer, half],
                        device_id={"col": peer},
                        device_id_type=MESH,
                    ).wait_recv()
            total[s] += dot(held[peer], column_in[s, 0, peer]) + dot(held[4 + peer], column_in[s, 1, peer])

    def factor(value, part, actions):
        rows, marks = row_blocks(value), row_blocks(identity(1.0))
        for i in inverse_factor(rows, marks):
            if i in actions:
                actions[i]()
        for t in range(16):
            inverse[part, pl.ds(8 * t, 8)] = marks[t]

    factor(gram[0] + identity(SHIFT), 0, {})
    front[...] = dot(own[:, :128], inverse[0], ((1,), (1,)), HIGHEST)
    b_own[0] = front[...].astype(BF16)
    met(peers)
    spread(0)
    corner[...] = dot(gram[1], inverse[0], ((1,), (1,)), HIGHEST)

    def begin():
        select(0)
        share(0, 0)
        rows_out(0)

    def relay():
        share(0, 1)

    factor(
        gram[2] + identity(SHIFT) - dot(corner[...], corner[...], ((1,), (1,)), HIGHEST), 1, {10: begin, 15: relay}
    )
    rest = own[:, 128:] - dot(front[...], corner[...], ((1,), (1,)), HIGHEST)
    b_own[1] = dot(rest, inverse[1], ((1,), (1,)), HIGHEST).astype(BF16)
    spread(1)
    share(0, 2)
    write_basis(0)
    select(1)
    share(1, 0)
    rows_out(1)
    share(0, 3)
    share(1, 1)
    share(0, 4)
    share(1, 2)
    write_basis(1)
    for load in loads:
        load.wait()
    share(1, 3)
    weigh_own(0)
    share(1, 4)
    weigh_own(1)
    weigh(0)
    weigh(1)
    for copy in row_copies:
        copy.wait_recv()

    sums[...] = jnp.zeros_like(sums)
    for offset in range(8):
        rows = pl.ds(128 * offset, 128)
        value = jnp.concatenate([total[0, rows], total[1, rows]], axis=1)
        high = value.astype(BF16)
        low = (value - high.astype(F32)).astype(BF16)
        spot = pl.ds(128 * (offset % 2), 128)
        left = jnp.concatenate([row_in[0, offset // 2, spot], row_in[1, offset // 2, spot]], axis=1)
        product = dot(left, high, ((0,), (0,))) + dot(left, low, ((0,), (0,)))
        near = lax.rem(lax.shift_right_logical(block_map[c, 8 * r + offset], 3), 4)
        for g in range(4):
            sums[g] += product * jnp.where(near == g, 1.0, 0.0)

    for g in range(2):
        quarters = sums[2 + g].astype(BF16).reshape(4, 4, 16, 256)
        for q in range(4):
            x_out[4 * g + q] = quarters[:, q]
    x_copies, copies = [], []
    for i in (2, 1, 3):
        peer = ring(k + i, 4)
        rows = pl.ds(pl.multiple_of(peer * 64, 64), 64)
        f_out[i - 1] = sums[:2, rows].astype(BF16)
        copies.append(send(f_out.at[i - 1], f_in.at[i - 1], f_send.at[i - 1], f_recv.at[i - 1], {"col": peer}))
    for i in (4, 3, 5, 2, 6, 1, 7):
        peer = ring(c + i, 8)
        x_copies.append(send(x_out.at[peer], x_in.at[c], x_send.at[i - 1], x_recv.at[i - 1], {"child": peer}))
    x_in[c] = x_out[c]
    value = sums[:2, pl.ds(pl.multiple_of(k * 64, 64), 64)]
    for copy, i in zip(copies, (2, 1, 3)):
        copy.wait_recv()
        value = value + f_in[i - 1].astype(F32)
    pending += copies
    g_out[...] = value.astype(BF16).reshape(8, 16, 256)
    g_copies = []
    for i in (4, 3, 5, 2, 6, 1, 7):
        peer = ring(c + i, 8)
        g_copies.append(send(g_out.at[peer], g_in.at[c], g_send.at[i - 1], g_recv.at[i - 1], {"child": peer}))
    g_in[c] = g_out[c]
    for copy in x_copies:
        copy.wait_recv()
    pending += x_copies
    v_sum[...] = jnp.sum(x_in[...].astype(F32), axis=0)
    v_out[...] = v_sum[...].astype(BF16)
    copies = []
    for i in (2, 1, 3):
        peer = ring(k + i, 4)
        copies.append(send(v_out.at[peer], v_in.at[i - 1], v_send.at[i - 1], v_recv.at[i - 1], {"col": peer}))
    for copy in g_copies:
        copy.wait_recv()
    pending += g_copies
    h_out[0] = jnp.sum(g_in[...].astype(F32), axis=0).astype(BF16)
    value = v_sum[k]
    for copy, i in zip(copies, (2, 1, 3)):
        copy.wait_recv()
        value = value + v_in[i - 1].astype(F32)
    pending += copies
    h_out[1] = value.astype(BF16)
    copies = []
    for i in (4, 3, 5, 2, 6, 1, 7):
        copies.append(send(h_out, h_in.at[c], h_send.at[i - 1], h_recv.at[i - 1], {"child": ring(c + i, 8)}))
    h_in[c] = h_out[...]
    for copy in copies:
        copy.wait_recv()
    pending += copies
    coupling_out[...] = h_in[...]
    for copy in pending:
        copy.wait_send()
    for peer, copy in forwards:
        pl.when(peer != k)(copy.wait_send)


def in_vmem():
    return pl.BlockSpec(memory_space=pltpu.VMEM)


def in_smem():
    return pl.BlockSpec(memory_space=pltpu.SMEM)


def sampled(schur, sketch, block_map):
    dma = pltpu.SemaphoreType.DMA
    return pl.pallas_call(
        sample_kernel,
        out_shape=(jax.ShapeDtypeStruct((128, 256), F32), jax.ShapeDtypeStruct((3, 128, 128), F32)),
        in_specs=[pl.BlockSpec(memory_space=pl.ANY), in_vmem(), in_smem()],
        out_specs=(in_vmem(), in_vmem()),
        scratch_shapes=[
            pltpu.VMEM((8, 1024, 256), BF16),
            pltpu.VMEM((256, 1024), BF16),
            pltpu.VMEM((8, 256, 256), F32),
            pltpu.VMEM((2, 2, 2, 4, 64, 256), BF16),
            pltpu.VMEM((2, 2, 2, 4, 64, 256), BF16),
            pltpu.VMEM((2, 8, 128, 256), BF16),
            pltpu.VMEM((2, 1024, 128), F32),
            pltpu.VMEM((2, 3, 256, 128), BF16),
            pltpu.VMEM((2, 3, 256, 128), BF16),
            pltpu.VMEM((2, 2, 128, 128), BF16),
            pltpu.VMEM((2, 8, 128, 128), BF16),
            pltpu.VMEM((2, 8, 128, 128), BF16),
            dma((8,)),
            dma((2, 2, 2, 4)), dma((2, 2, 2, 4)),
            dma((2, 2, 2, 4)), dma((2, 2, 2, 4)),
            dma((2, 3)), dma((2, 3)),
            dma((2, 7)), dma((2, 7)),
            dma((2, 8)), dma((2, 8)),
        ],
        compiler_params=pltpu.CompilerParams(
            collective_id=0, has_side_effects=True, vmem_limit_bytes=VMEM_LIMIT
        ),
        name="samples",
    )(schur, sketch, block_map)


def coupled(schur, own, gram, block_map):
    dma = pltpu.SemaphoreType.DMA
    return pl.pallas_call(
        coupling_kernel,
        out_shape=(
            jax.ShapeDtypeStruct((2, 8, 128, 128), BF16),
            jax.ShapeDtypeStruct((8, 2, 16, 256), BF16),
        ),
        in_specs=[pl.BlockSpec(memory_space=pl.ANY), in_vmem(), in_vmem(), in_smem()],
        out_specs=(in_vmem(), in_vmem()),
        scratch_shapes=[
            pltpu.VMEM((8, 1024, 256), BF16),
            pltpu.VMEM((2, 128, 128), F32),
            pltpu.VMEM((128, 128), F32),
            pltpu.VMEM((128, 128), F32),
            pltpu.VMEM((2, 128, 128), BF16),
            pltpu.VMEM((8, 128, 128), BF16),
            pltpu.VMEM((8, 128, 128), BF16),
            pltpu.VMEM((2, 8, 256, 128), BF16),
            pltpu.VMEM((2, 2, 4, 256, 128), BF16),
            pltpu.VMEM((2, 4, 256, 128), BF16),
            pltpu.VMEM((2, 1024, 128), F32),
            pltpu.VMEM((4, 256, 256), F32),
            pltpu.VMEM((3, 2, 64, 256), BF16),
            pltpu.VMEM((3, 2, 64, 256), BF16),
            pltpu.VMEM((8, 4, 16, 256), BF16),
            pltpu.VMEM((8, 4, 16, 256), BF16),
            pltpu.VMEM((8, 16, 256), BF16),
            pltpu.VMEM((8, 16, 256), BF16),
            pltpu.VMEM((4, 16, 256), F32),
            pltpu.VMEM((4, 16, 256), BF16),
            pltpu.VMEM((3, 16, 256), BF16),
            pltpu.VMEM((2, 16, 256), BF16),
            pltpu.VMEM((8, 2, 16, 256), BF16),
            dma((8,)),
            dma((2, 7)), dma((2, 7)),
            dma((2, 2, 2, 4)), dma((2, 2, 2, 4)),
            dma((2, 8, 2)), dma((2, 2, 4, 2)),
            dma((2, 3)), dma((2, 3)),
            dma((3,)), dma((3,)),
            dma((7,)), dma((7,)),
            dma((7,)), dma((7,)),
            dma((3,)), dma((3,)),
            dma((7,)), dma((7,)),
        ],
        compiler_params=pltpu.CompilerParams(
            collective_id=1, has_side_effects=True, vmem_limit_bytes=VMEM_LIMIT
        ),
        name="coupling",
    )(schur, own, gram, block_map)


def place_kernel(basis, coupling, owner_slot, basis_out, coupling_out):
    c, r = lax.axis_index("child"), lax.axis_index("row")
    for slot in range(2):
        share = [jnp.where(owner_slot[4 * r + g] == 2 * c + slot, 1.0, 0.0) for g in range(4)]
        for half in range(2):
            for s in range(2):
                value = basis[s, half].astype(F32) * share[0]
                for g in range(1, 4):
                    value = value + basis[s, 2 * g + half].astype(F32) * share[g]
                basis_out[slot, 0, pl.ds(128 * half, 128), pl.ds(128 * s, 128)] = value
        for q in range(4):
            value = coupling[q, 0].astype(F32) * share[0]
            for g in range(1, 4):
                value = value + coupling[4 * (g % 2) + q, g // 2].astype(F32) * share[g]
            coupling_out[slot, 0, pl.ds(16 * q, 16)] = value


def placed_results(basis, coupling, owner_slot):
    return pl.pallas_call(
        place_kernel,
        out_shape=(
            jax.ShapeDtypeStruct((2, 1, 256, 256), F32),
            jax.ShapeDtypeStruct((2, 1, 64, 256), F32),
        ),
        in_specs=[in_vmem(), in_vmem(), in_smem()],
        out_specs=(in_vmem(), in_vmem()),
        name="results",
    )(basis, coupling, owner_slot)


def shards(schur_blocks, sketch_cols, block_map, owner_slot):
    own, gram = sampled(schur_blocks, sketch_cols, block_map)
    basis, coupling = coupled(schur_blocks, own, gram, block_map)
    return placed_results(basis, coupling, owner_slot)


def solution(mesh):
    placed = (P("child", "row", "col"), P("row", None), P(), P())
    return jax.shard_map(
        shards,
        mesh=mesh,
        in_specs=placed,
        out_specs=(P("child", "row", "col", None), P("child", "row", "col", None)),
        check_vma=False,
    )
```

```python
import functools

import jax
import jax.numpy as jnp
from jax import lax
from jax.experimental import pallas as pl
from jax.experimental.pallas import tpu as pltpu
from jax.sharding import PartitionSpec as P

MESH = pl.DeviceIdType.MESH
F32, BF16 = jnp.float32, jnp.bfloat16
HIGHEST = lax.Precision.HIGHEST
VMEM_LIMIT = 60 * 1024 * 1024
SHIFT = 64.0


def ring(value, size):
    return lax.rem(value + 2 * size, size)


def dot(left, right, dims=((1,), (0,)), precision=None):
    return lax.dot_general(left, right, (dims, ((), ())), precision=precision, preferred_element_type=F32)


def hello(peers):
    for peer in peers:
        pl.semaphore_signal(pltpu.get_barrier_semaphore(), inc=1, device_id=peer, device_id_type=MESH)


def met(peers):
    pl.semaphore_wait(pltpu.get_barrier_semaphore(), len(peers))


def send(source, target, send_sem, recv_sem, peer):
    copy = pltpu.make_async_remote_copy(
        src_ref=source,
        dst_ref=target,
        send_sem=send_sem,
        recv_sem=recv_sem,
        device_id=peer,
        device_id_type=MESH,
    )
    copy.start()
    return copy


def place():
    return lax.axis_index("child"), lax.axis_index("row"), lax.axis_index("col")


def columns(chunk):
    return pl.ds(pl.multiple_of(chunk * 256, 256), 256)


def lanes(value, column):
    return jnp.broadcast_to(value[:, column : column + 1], (8, 128))


def sublanes(value, row):
    return jnp.broadcast_to(value[row : row + 1, :], (8, 128))


def inverse_factor(rows, marks):
    sub = lax.broadcasted_iota(jnp.int32, (8, 128), 0)
    for i in range(16):
        left = [[lanes(rows[t], 8 * i + p) for p in range(8)] for t in range(i, 16)]
        inner = {(q, p): sublanes(left[0][p], q) for p in range(8) for q in range(p, 8)}
        upper = [sublanes(rows[i], p) for p in range(8)]
        done = [sublanes(marks[i], p) for p in range(8)]
        for p in range(8):
            scale = lax.rsqrt(inner[p, p])
            for q in range(p + 1, 8):
                inner[q, p] = inner[q, p] * scale
            upper[p] = upper[p] * scale
            done[p] = done[p] * scale
            for t in range(1, 16 - i):
                left[t][p] = left[t][p] * scale
            for q in range(p + 1, 8):
                for s in range(q, 8):
                    inner[s, q] = inner[s, q] - inner[s, p] * inner[q, p]
                upper[q] = upper[q] - inner[q, p] * upper[p]
                done[q] = done[q] - inner[q, p] * done[p]
                for t in range(1, 16 - i):
                    left[t][q] = left[t][q] - left[t][p] * inner[q, p]
        for t in range(1, 16 - i):
            for p in range(8):
                if i + 1 < 16:
                    rows[i + t] = rows[i + t] - left[t][p] * upper[p]
                marks[i + t] = marks[i + t] - left[t][p] * done[p]
        value = done[0]
        for p in range(1, 8):
            value = jnp.where(sub == p, done[p], value)
        marks[i] = value
        yield i


def row_blocks(value):
    return [value[8 * t : 8 * t + 8] for t in range(16)]


def identity(scale):
    row = lax.broadcasted_iota(jnp.int32, (128, 128), 0)
    column = lax.broadcasted_iota(jnp.int32, (128, 128), 1)
    return jnp.where(row == column, scale, 0.0)


def sample_steps(
    schur, sketch, block_map, own_out, gram_out,
    held, turned, part, sums_out, sums_in, power, total, b_out, b_in, c_out, c_in, z_all,
    load_sem, a_send, a_recv, p_send, p_recv, b_send, b_recv, c_send, c_recv, z_send, z_recv,
):
    c, r, k = place()
    pair, core = lax.div(c, 2), lax.rem(c, 2)
    below, above = {"row": ring(r - 1, 8)}, {"row": ring(r + 1, 8)}
    siblings = [{"child": ring(c + i, 8)} for i in range(1, 8)]
    group = [{"col": ring(k + i, 4)} for i in range(1, 4)]
    cross = [{"child": 2 * pair + 1 - core, "col": ring(k + i, 4)} for i in range(1, 4)]
    peers = [below, above] + siblings + group + cross
    hello(peers)
    loads = {}
    for spot, rel in enumerate((4, 5, 3, 6, 2, 7, 1, 0)):
        chunk = ring(r + rel, 8)
        loads[rel] = pltpu.make_async_copy(schur.at[0, :, columns(chunk)], held.at[chunk], load_sem.at[spot])
        loads[rel].start()
    turned[...] = sketch[...].T

    def produce(rel):
        chunk = ring(r + rel, 8)
        loads[rel].wait()
        part[chunk] = dot(turned[...], held[chunk])

    pending = []
    arriving = {}
    lanesets = ((0, 0), (1, 1), (0, 1), (1, 0))

    def pass_on(s, way, u, step):
        hops = 4 - u if way == 0 else 3 + u
        if step >= hops:
            return
        chunk = ring(r - hops + step if way == 0 else r + hops - step, 8)
        value = part[chunk, pl.ds(128 * s + 64 * u, 64)]
        if step:
            arriving[s, way, u, step - 1].wait_recv()
            value = value + sums_in[s, way, u, step - 1].astype(F32)
        sums_out[s, way, u, step] = value.astype(BF16)
        copy = send(
            sums_out.at[s, way, u, step], sums_in.at[s, way, u, step],
            a_send.at[s, way, u, step], a_recv.at[s, way, u, step], below if way == 0 else above,
        )
        arriving[s, way, u, step] = copy
        pending.append(copy)

    produce(4)
    met(peers)
    for s in range(2):
        pass_on(s, 0, 0, 0)
        pass_on(s, 1, 1, 0)
    produce(5)
    for s in range(2):
        pass_on(s, 0, 1, 0)
    produce(3)
    for s in range(2):
        pass_on(s, 1, 0, 0)
    for step, rels in ((1, (6, 2)), (2, (7, 1)), (3, (0,))):
        for rel in rels:
            produce(rel)
        for s in range(2):
            for way, u in lanesets:
                pass_on(s, way, u, step)

    def finish_sum(s):
        for u in range(2):
            value = part[r, pl.ds(128 * s + 64 * u, 64)]
            for way, hops in ((0, 4 - u), (1, 3 + u)):
                arriving[s, way, u, hops - 1].wait_recv()
                value = value + sums_in[s, way, u, hops - 1].astype(F32)
            power[s, r, pl.ds(64 * u, 64)] = value.astype(BF16)

    coming = {}

    def share(s, way, u, step):
        hops = 4 - u if way == 0 else 3 + u
        if step and step <= hops:
            coming[s, way, u, step - 1].wait_recv()
        if step >= hops:
            return
        chunk = ring(r - step if way == 0 else r + step, 8)
        ref = power.at[s, chunk, pl.ds(64 * u, 64)]
        copy = send(
            ref, ref, p_send.at[s, way, u, step], p_recv.at[s, way, u, step], above if way == 0 else below
        )
        coming[s, way, u, step] = copy
        pending.append(copy)

    def multiply(s, chunk):
        return dot(held[chunk], power[s, chunk], ((1,), (1,)))

    for s in range(2):
        finish_sum(s)
        for way, u in lanesets:
            share(s, way, u, 0)
    for s in range(2):
        total[s] = multiply(s, r)
    for step in range(1, 4):
        for s in range(2):
            for way, u in lanesets:
                share(s, way, u, step)
            total[s] += multiply(s, ring(r - step, 8)) + multiply(s, ring(r + step, 8))

    last = ring(r + 4, 8)
    summed, sent = {}, {}
    for s in range(2):
        share(s, 0, 0, 4)
        share(s, 1, 1, 4)
        sent[s] = []
        for i in (2, 1, 3, 0):
            peer = ring(k + i, 4)
            rows = pl.ds(pl.multiple_of(peer * 256, 256), 256)
            value = total[s, rows] + dot(held[last, rows], power[s, last], ((1,), (1,)))
            if i:
                b_out[s, i - 1] = value.astype(BF16)
                copy = send(
                    b_out.at[s, i - 1], b_in.at[s, i - 1], b_send.at[s, i - 1], b_recv.at[s, i - 1], {"col": peer}
                )
                sent[s].append((i, copy))
                pending.append(copy)
            else:
                total[s, rows] = value

    swapped = {}
    for s in range(2):
        value = total[s, pl.ds(pl.multiple_of(k * 256, 256), 256)]
        for i, copy in sent[s]:
            copy.wait_recv()
            value = value + b_in[s, i - 1].astype(F32)
        c_out[s] = value.astype(BF16).reshape(2, 128, 128)
        swapped[s] = []
        for i in (4, 3, 5, 2, 6, 1, 7):
            peer = ring(c + i, 8)
            copy = send(
                c_out.at[s, lax.rem(peer, 2)], c_in.at[s, c], c_send.at[s, i - 1], c_recv.at[s, i - 1], {"child": peer}
            )
            swapped[s].append(copy)
            pending.append(copy)
        c_in[s, c] = c_out[s, core]

    spot = 8 * r + 2 * k + core
    offset = 2 * k + core
    gathered = {}
    for s in range(2):
        for copy in swapped[s]:
            copy.wait_recv()
        value = jnp.zeros((128, 128), F32)
        for child in range(8):
            wanted = lax.shift_right_logical(block_map[child, spot], 3) == 4 * r + pair
            value = value + c_in[s, child].astype(F32) * jnp.where(wanted, 1.0, 0.0)
        own_out[:, pl.ds(128 * s, 128)] = value
        z_all[s, offset] = value.astype(BF16)
        gathered[s] = []
        ref = z_all.at[s, offset]
        for i in (2, 1, 3, 0):
            for other in range(2):
                if i == 0 and other == 0:
                    continue
                slot = 2 * i + other
                copy = send(
                    ref, ref, z_send.at[s, slot], z_recv.at[s, slot],
                    {"child": c if other == 0 else 2 * pair + 1 - core, "col": ring(k + i, 4)},
                )
                gathered[s].append(copy)
                pending.append(copy)
    for copy in gathered[0]:
        copy.wait_recv()
    first = z_all[0].reshape(1024, 128)
    gram_out[0] = dot(first, first, ((0,), (0,)))
    yield
    for copy in gathered[1]:
        copy.wait_recv()
    second = z_all[1].reshape(1024, 128)
    gram_out[1] = dot(second, first, ((0,), (0,)))
    gram_out[2] = dot(second, second, ((0,), (0,)))
    for copy in pending:
        copy.wait_send()


def coupling_steps(
    sampling, own, gram, block_map, basis_out, coupling_out,
    held, inverse, corner, front, b_own, e_low, e_high, mine, column_in, row_in, total, sums,
    f_out, f_in, x_out, x_in, g_out, g_in, v_sum, v_out, v_in, h_out, h_in,
    e_send, e_recv, z_send, z_recv, y_send, y_recv, r_send, r_recv, f_send, f_recv, x_send, x_recv,
    g_send, g_recv, v_send, v_recv, h_send, h_recv,
):
    c, r, k = place()
    below, above = {"row": ring(r - 1, 8)}, {"row": ring(r + 1, 8)}
    pending = []
    outgoing = {}
    e_in = (e_low, e_high)

    def spread(s):
        outgoing[s] = []
        for i in (4, 3, 5, 2, 6, 1, 7):
            copy = send(
                b_own.at[s], e_in[s].at[c], e_send.at[s, i - 1], e_recv.at[s, i - 1], {"child": ring(c + i, 8)}
            )
            outgoing[s].append(copy)
            pending.append(copy)
        e_in[s][c] = b_own[s]

    def select(s):
        for copy in outgoing[s]:
            copy.wait_recv()
        for half in range(2):
            near = lax.rem(lax.shift_right_logical(block_map[c, 8 * r + 2 * k + half], 3), 4)
            mine[s, r, pl.ds(128 * half, 128)] = e_in[s][2 * near + half]

    arriving = {}
    forwards = []
    lanesets = ((0, 0), (1, 1), (0, 1), (1, 0))

    def across(s, rel, half):
        chunk = ring(r + rel, 8)
        peer = lax.div(chunk, 2)
        copy = pltpu.make_async_remote_copy(
            src_ref=mine.at[s, chunk, pl.ds(128 * half, 128)],
            dst_ref=column_in.at[s, lax.rem(chunk, 2), k, pl.ds(128 * half, 128)],
            send_sem=y_send.at[s, rel, half],
            recv_sem=y_recv.at[s, lax.rem(chunk, 2), k, half],
            device_id={"col": peer},
            device_id_type=MESH,
        )
        pl.when(peer != k)(copy.start)
        forwards.append((peer, copy))

    def share(s, step):
        for way, half in lanesets:
            hops = 4 - half if way == 0 else 3 + half
            if step > hops:
                continue
            if step:
                arriving[s, way, half, step - 1].wait_recv()
            if step < hops:
                chunk = ring(r - step if way == 0 else r + step, 8)
                ref = mine.at[s, chunk, pl.ds(128 * half, 128)]
                copy = send(
                    ref, ref, z_send.at[s, way, half, step], z_recv.at[s, way, half, step],
                    above if way == 0 else below,
                )
                arriving[s, way, half, step] = copy
                pending.append(copy)
            if step:
                across(s, (8 - step if way == 0 else step) % 8, half)
        if step == 0:
            for half in range(2):
                across(s, 0, half)

    row_copies = []

    def rows_out(s):
        for i in (2, 1, 3):
            copy = send(
                mine.at[s, r], row_in.at[s, k], r_send.at[s, i - 1], r_recv.at[s, i - 1], {"col": ring(k + i, 4)}
            )
            row_copies.append(copy)
            pending.append(copy)
        row_in[s, k] = mine[s, r]

    def write_basis(s):
        basis_out[s] = e_in[s][...]

    def weigh_own(s):
        total[s] = dot(held[k], mine[s, 2 * k]) + dot(held[4 + k], mine[s, 2 * k + 1])

    def weigh(s):
        for i in (1, 3, 2):
            peer = ring(k + i, 4)
            for odd in range(2):
                for half in range(2):
                    pltpu.make_async_remote_copy(
                        src_ref=mine.at[s, 0, pl.ds(128 * half, 128)],
                        dst_ref=column_in.at[s, odd, peer, pl.ds(128 * half, 128)],
                        send_sem=y_send.at[s, 0, half],
                        recv_sem=y_recv.at[s, odd, peer, half],
                        device_id={"col": peer},
                        device_id_type=MESH,
                    ).wait_recv()
            total[s] += dot(held[peer], column_in[s, 0, peer]) + dot(held[4 + peer], column_in[s, 1, peer])

    def factor(value, part, actions):
        rows, marks = row_blocks(value), row_blocks(identity(1.0))
        for i in inverse_factor(rows, marks):
            if i in actions:
                actions[i]()
        for t in range(16):
            inverse[part, pl.ds(8 * t, 8)] = marks[t]

    factor(gram[0] + identity(SHIFT), 0, {})
    front[...] = dot(own[:, :128], inverse[0], ((1,), (1,)), HIGHEST)
    b_own[0] = front[...].astype(BF16)
    spread(0)
    for _ in sampling:
        pass
    corner[...] = dot(gram[1], inverse[0], ((1,), (1,)), HIGHEST)

    def begin():
        select(0)
        share(0, 0)
        rows_out(0)

    def relay():
        share(0, 1)

    factor(
        gram[2] + identity(SHIFT) - dot(corner[...], corner[...], ((1,), (1,)), HIGHEST), 1, {10: begin, 15: relay}
    )
    rest = own[:, 128:] - dot(front[...], corner[...], ((1,), (1,)), HIGHEST)
    b_own[1] = dot(rest, inverse[1], ((1,), (1,)), HIGHEST).astype(BF16)
    spread(1)
    share(0, 2)
    write_basis(0)
    select(1)
    share(1, 0)
    rows_out(1)
    share(0, 3)
    share(1, 1)
    share(0, 4)
    share(1, 2)
    write_basis(1)
    share(1, 3)
    weigh_own(0)
    share(1, 4)
    weigh_own(1)
    weigh(0)
    weigh(1)
    for copy in row_copies:
        copy.wait_recv()

    sums[...] = jnp.zeros_like(sums)
    for offset in range(8):
        rows = pl.ds(128 * offset, 128)
        value = jnp.concatenate([total[0, rows], total[1, rows]], axis=1)
        high = value.astype(BF16)
        low = (value - high.astype(F32)).astype(BF16)
        spot = pl.ds(128 * (offset % 2), 128)
        left = jnp.concatenate([row_in[0, offset // 2, spot], row_in[1, offset // 2, spot]], axis=1)
        product = dot(left, high, ((0,), (0,))) + dot(left, low, ((0,), (0,)))
        near = lax.rem(lax.shift_right_logical(block_map[c, 8 * r + offset], 3), 4)
        for g in range(4):
            sums[g] += product * jnp.where(near == g, 1.0, 0.0)

    for g in range(2):
        quarters = sums[2 + g].astype(BF16).reshape(4, 4, 16, 256)
        for q in range(4):
            x_out[4 * g + q] = quarters[:, q]
    x_copies, copies = [], []
    for i in (2, 1, 3):
        peer = ring(k + i, 4)
        rows = pl.ds(pl.multiple_of(peer * 64, 64), 64)
        f_out[i - 1] = sums[:2, rows].astype(BF16)
        copies.append(send(f_out.at[i - 1], f_in.at[i - 1], f_send.at[i - 1], f_recv.at[i - 1], {"col": peer}))
    for i in (4, 3, 5, 2, 6, 1, 7):
        peer = ring(c + i, 8)
        x_copies.append(send(x_out.at[peer], x_in.at[c], x_send.at[i - 1], x_recv.at[i - 1], {"child": peer}))
    x_in[c] = x_out[c]
    value = sums[:2, pl.ds(pl.multiple_of(k * 64, 64), 64)]
    for copy, i in zip(copies, (2, 1, 3)):
        copy.wait_recv()
        value = value + f_in[i - 1].astype(F32)
    pending += copies
    g_out[...] = value.astype(BF16).reshape(8, 16, 256)
    g_copies = []
    for i in (4, 3, 5, 2, 6, 1, 7):
        peer = ring(c + i, 8)
        g_copies.append(send(g_out.at[peer], g_in.at[c], g_send.at[i - 1], g_recv.at[i - 1], {"child": peer}))
    g_in[c] = g_out[c]
    for copy in x_copies:
        copy.wait_recv()
    pending += x_copies
    v_sum[...] = jnp.sum(x_in[...].astype(F32), axis=0)
    v_out[...] = v_sum[...].astype(BF16)
    copies = []
    for i in (2, 1, 3):
        peer = ring(k + i, 4)
        copies.append(send(v_out.at[peer], v_in.at[i - 1], v_send.at[i - 1], v_recv.at[i - 1], {"col": peer}))
    for copy in g_copies:
        copy.wait_recv()
    pending += g_copies
    h_out[0] = jnp.sum(g_in[...].astype(F32), axis=0).astype(BF16)
    value = v_sum[k]
    for copy, i in zip(copies, (2, 1, 3)):
        copy.wait_recv()
        value = value + v_in[i - 1].astype(F32)
    pending += copies
    h_out[1] = value.astype(BF16)
    copies = []
    for i in (4, 3, 5, 2, 6, 1, 7):
        copies.append(send(h_out, h_in.at[c], h_send.at[i - 1], h_recv.at[i - 1], {"child": ring(c + i, 8)}))
    h_in[c] = h_out[...]
    for copy in copies:
        copy.wait_recv()
    pending += copies
    coupling_out[...] = h_in[...]
    for copy in pending:
        copy.wait_send()
    for peer, copy in forwards:
        pl.when(peer != k)(copy.wait_send)


def whole_kernel(schur, sketch, block_map, basis_out, coupling_out, own, gram, held, *rest):
    sampling = sample_steps(schur, sketch, block_map, own, gram, held, *rest[:22])
    next(sampling)
    coupling_steps(sampling, own, gram, block_map, basis_out, coupling_out, held, *rest[22:])


def in_vmem():
    return pl.BlockSpec(memory_space=pltpu.VMEM)


def in_smem():
    return pl.BlockSpec(memory_space=pltpu.SMEM)


def solved(schur, sketch, block_map):
    dma = pltpu.SemaphoreType.DMA
    return pl.pallas_call(
        whole_kernel,
        out_shape=(
            jax.ShapeDtypeStruct((2, 8, 128, 128), BF16),
            jax.ShapeDtypeStruct((8, 2, 16, 256), BF16),
        ),
        in_specs=[pl.BlockSpec(memory_space=pl.ANY), in_vmem(), in_smem()],
        out_specs=(in_vmem(), in_vmem()),
        scratch_shapes=[
            pltpu.VMEM((128, 256), F32),
            pltpu.VMEM((3, 128, 128), F32),
            pltpu.VMEM((8, 1024, 256), BF16),
            pltpu.VMEM((256, 1024), BF16),
            pltpu.VMEM((8, 256, 256), F32),
            pltpu.VMEM((2, 2, 2, 4, 64, 256), BF16),
            pltpu.VMEM((2, 2, 2, 4, 64, 256), BF16),
            pltpu.VMEM((2, 8, 128, 256), BF16),
            pltpu.VMEM((2, 1024, 128), F32),
            pltpu.VMEM((2, 3, 256, 128), BF16),
            pltpu.VMEM((2, 3, 256, 128), BF16),
            pltpu.VMEM((2, 2, 128, 128), BF16),
            pltpu.VMEM((2, 8, 128, 128), BF16),
            pltpu.VMEM((2, 8, 128, 128), BF16),
            dma((8,)),
            dma((2, 2, 2, 4)), dma((2, 2, 2, 4)),
            dma((2, 2, 2, 4)), dma((2, 2, 2, 4)),
            dma((2, 3)), dma((2, 3)),
            dma((2, 7)), dma((2, 7)),
            dma((2, 8)), dma((2, 8)),
            pltpu.VMEM((2, 128, 128), F32),
            pltpu.VMEM((128, 128), F32),
            pltpu.VMEM((128, 128), F32),
            pltpu.VMEM((2, 128, 128), BF16),
            pltpu.VMEM((8, 128, 128), BF16),
            pltpu.VMEM((8, 128, 128), BF16),
            pltpu.VMEM((2, 8, 256, 128), BF16),
            pltpu.VMEM((2, 2, 4, 256, 128), BF16),
            pltpu.VMEM((2, 4, 256, 128), BF16),
            pltpu.VMEM((2, 1024, 128), F32),
            pltpu.VMEM((4, 256, 256), F32),
            pltpu.VMEM((3, 2, 64, 256), BF16),
            pltpu.VMEM((3, 2, 64, 256), BF16),
            pltpu.VMEM((8, 4, 16, 256), BF16),
            pltpu.VMEM((8, 4, 16, 256), BF16),
            pltpu.VMEM((8, 16, 256), BF16),
            pltpu.VMEM((8, 16, 256), BF16),
            pltpu.VMEM((4, 16, 256), F32),
            pltpu.VMEM((4, 16, 256), BF16),
            pltpu.VMEM((3, 16, 256), BF16),
            pltpu.VMEM((2, 16, 256), BF16),
            pltpu.VMEM((8, 2, 16, 256), BF16),
            dma((2, 7)), dma((2, 7)),
            dma((2, 2, 2, 4)), dma((2, 2, 2, 4)),
            dma((2, 8, 2)), dma((2, 2, 4, 2)),
            dma((2, 3)), dma((2, 3)),
            dma((3,)), dma((3,)),
            dma((7,)), dma((7,)),
            dma((7,)), dma((7,)),
            dma((3,)), dma((3,)),
            dma((7,)), dma((7,)),
        ],
        compiler_params=pltpu.CompilerParams(
            collective_id=0, has_side_effects=True, vmem_limit_bytes=VMEM_LIMIT
        ),
        name="basis_step",
    )(schur, sketch, block_map)


def place_kernel(basis, coupling, owner_slot, basis_out, coupling_out):
    c, r = lax.axis_index("child"), lax.axis_index("row")
    for slot in range(2):
        share = [jnp.where(owner_slot[4 * r + g] == 2 * c + slot, 1.0, 0.0) for g in range(4)]
        for half in range(2):
            for s in range(2):
                value = basis[s, half].astype(F32) * share[0]
                for g in range(1, 4):
                    value = value + basis[s, 2 * g + half].astype(F32) * share[g]
                basis_out[slot, 0, pl.ds(128 * half, 128), pl.ds(128 * s, 128)] = value
        for q in range(4):
            value = coupling[q, 0].astype(F32) * share[0]
            for g in range(1, 4):
                value = value + coupling[4 * (g % 2) + q, g // 2].astype(F32) * share[g]
            coupling_out[slot, 0, pl.ds(16 * q, 16)] = value


def placed_results(basis, coupling, owner_slot):
    return pl.pallas_call(
        place_kernel,
        out_shape=(
            jax.ShapeDtypeStruct((2, 1, 256, 256), F32),
            jax.ShapeDtypeStruct((2, 1, 64, 256), F32),
        ),
        in_specs=[in_vmem(), in_vmem(), in_smem()],
        out_specs=(in_vmem(), in_vmem()),
        name="results",
    )(basis, coupling, owner_slot)


def shards(schur_blocks, sketch_cols, block_map, owner_slot):
    basis, coupling = solved(schur_blocks, sketch_cols, block_map)
    return placed_results(basis, coupling, owner_slot)


def solution(mesh):
    placed = (P("child", "row", "col"), P("row", None), P(), P())
    return jax.shard_map(
        shards,
        mesh=mesh,
        in_specs=placed,
        out_specs=(P("child", "row", "col", None), P("child", "row", "col", None)),
        check_vma=False,
    )
```

```python
import functools

import jax
import jax.numpy as jnp
from jax import lax
from jax.experimental import pallas as pl
from jax.experimental.pallas import tpu as pltpu
from jax.sharding import PartitionSpec as P

MESH = pl.DeviceIdType.MESH
F32, BF16 = jnp.float32, jnp.bfloat16
HIGHEST = lax.Precision.HIGHEST
VMEM_LIMIT = 60 * 1024 * 1024
SHIFT = 64.0


def ring(value, size):
    return lax.rem(value + 2 * size, size)


def dot(left, right, dims=((1,), (0,)), precision=None):
    return lax.dot_general(left, right, (dims, ((), ())), precision=precision, preferred_element_type=F32)


def hello(peers):
    for peer in peers:
        pl.semaphore_signal(pltpu.get_barrier_semaphore(), inc=1, device_id=peer, device_id_type=MESH)


def met(peers):
    pl.semaphore_wait(pltpu.get_barrier_semaphore(), len(peers))


def send(source, target, send_sem, recv_sem, peer):
    copy = pltpu.make_async_remote_copy(
        src_ref=source,
        dst_ref=target,
        send_sem=send_sem,
        recv_sem=recv_sem,
        device_id=peer,
        device_id_type=MESH,
    )
    copy.start()
    return copy


def place():
    return lax.axis_index("child"), lax.axis_index("row"), lax.axis_index("col")


def columns(chunk):
    return pl.ds(pl.multiple_of(chunk * 256, 256), 256)


def lanes(value, column):
    return jnp.broadcast_to(value[:, column : column + 1], (8, 128))


def sublanes(value, row):
    return jnp.broadcast_to(value[row : row + 1, :], (8, 128))


def inverse_factor(rows, marks):
    sub = lax.broadcasted_iota(jnp.int32, (8, 128), 0)
    for i in range(16):
        left = [[lanes(rows[t], 8 * i + p) for p in range(8)] for t in range(i, 16)]
        inner = {(q, p): sublanes(left[0][p], q) for p in range(8) for q in range(p, 8)}
        upper = [sublanes(rows[i], p) for p in range(8)]
        done = [sublanes(marks[i], p) for p in range(8)]
        for p in range(8):
            scale = lax.rsqrt(inner[p, p])
            for q in range(p + 1, 8):
                inner[q, p] = inner[q, p] * scale
            upper[p] = upper[p] * scale
            done[p] = done[p] * scale
            for t in range(1, 16 - i):
                left[t][p] = left[t][p] * scale
            for q in range(p + 1, 8):
                for s in range(q, 8):
                    inner[s, q] = inner[s, q] - inner[s, p] * inner[q, p]
                upper[q] = upper[q] - inner[q, p] * upper[p]
                done[q] = done[q] - inner[q, p] * done[p]
                for t in range(1, 16 - i):
                    left[t][q] = left[t][q] - left[t][p] * inner[q, p]
        for t in range(1, 16 - i):
            for p in range(8):
                if i + 1 < 16:
                    rows[i + t] = rows[i + t] - left[t][p] * upper[p]
                marks[i + t] = marks[i + t] - left[t][p] * done[p]
        value = done[0]
        for p in range(1, 8):
            value = jnp.where(sub == p, done[p], value)
        marks[i] = value
        yield i


def row_blocks(value):
    return [value[8 * t : 8 * t + 8] for t in range(16)]


def identity(scale):
    row = lax.broadcasted_iota(jnp.int32, (128, 128), 0)
    column = lax.broadcasted_iota(jnp.int32, (128, 128), 1)
    return jnp.where(row == column, scale, 0.0)


def sample_steps(
    schur, sketch, block_map, own_out, gram_out,
    held, turned, part, sums_out, sums_in, power, total, b_out, b_in, c_out, c_in, z_all,
    load_sem, a_send, a_recv, p_send, p_recv, b_send, b_recv, c_send, c_recv, z_send, z_recv,
):
    c, r, k = place()
    pair, core = lax.div(c, 2), lax.rem(c, 2)
    below, above = {"row": ring(r - 1, 8)}, {"row": ring(r + 1, 8)}
    siblings = [{"child": ring(c + i, 8)} for i in range(1, 8)]
    group = [{"col": ring(k + i, 4)} for i in range(1, 4)]
    cross = [{"child": 2 * pair + 1 - core, "col": ring(k + i, 4)} for i in range(1, 4)]
    peers = [below, above] + siblings + group + cross
    hello(peers)
    loads = {}
    for spot, rel in enumerate((4, 5, 3, 6, 2, 7, 1, 0)):
        chunk = ring(r + rel, 8)
        loads[rel] = pltpu.make_async_copy(schur.at[0, :, columns(chunk)], held.at[chunk], load_sem.at[spot])
        loads[rel].start()
    turned[...] = sketch[...].T

    def produce(rel):
        chunk = ring(r + rel, 8)
        loads[rel].wait()
        part[chunk] = dot(turned[...], held[chunk])

    pending = []
    arriving = {}
    lanesets = ((0, 0), (1, 1), (0, 1), (1, 0))

    def pass_on(s, way, u, step):
        hops = 4 - u if way == 0 else 3 + u
        if step >= hops:
            return
        chunk = ring(r - hops + step if way == 0 else r + hops - step, 8)
        value = part[chunk, pl.ds(128 * s + 64 * u, 64)]
        if step:
            arriving[s, way, u, step - 1].wait_recv()
            value = value + sums_in[s, way, u, step - 1].astype(F32)
        sums_out[s, way, u, step] = value.astype(BF16)
        copy = send(
            sums_out.at[s, way, u, step], sums_in.at[s, way, u, step],
            a_send.at[s, way, u, step], a_recv.at[s, way, u, step], below if way == 0 else above,
        )
        arriving[s, way, u, step] = copy
        pending.append(copy)

    produce(4)
    met(peers)
    for s in range(2):
        pass_on(s, 0, 0, 0)
        pass_on(s, 1, 1, 0)
    produce(5)
    for s in range(2):
        pass_on(s, 0, 1, 0)
    produce(3)
    for s in range(2):
        pass_on(s, 1, 0, 0)
    for step, rels in ((1, (6, 2)), (2, (7, 1)), (3, (0,))):
        for rel in rels:
            produce(rel)
        for s in range(2):
            for way, u in lanesets:
                pass_on(s, way, u, step)

    def finish_sum(s):
        for u in range(2):
            value = part[r, pl.ds(128 * s + 64 * u, 64)]
            for way, hops in ((0, 4 - u), (1, 3 + u)):
                arriving[s, way, u, hops - 1].wait_recv()
                value = value + sums_in[s, way, u, hops - 1].astype(F32)
            power[s, r, pl.ds(64 * u, 64)] = value.astype(BF16)

    coming = {}

    def share(s, way, u, step):
        hops = 4 - u if way == 0 else 3 + u
        if step and step <= hops:
            coming[s, way, u, step - 1].wait_recv()
        if step >= hops:
            return
        chunk = ring(r - step if way == 0 else r + step, 8)
        ref = power.at[s, chunk, pl.ds(64 * u, 64)]
        copy = send(
            ref, ref, p_send.at[s, way, u, step], p_recv.at[s, way, u, step], above if way == 0 else below
        )
        coming[s, way, u, step] = copy
        pending.append(copy)

    def multiply(s, chunk):
        return dot(held[chunk], power[s, chunk], ((1,), (1,)))

    for s in range(2):
        finish_sum(s)
        for way, u in lanesets:
            share(s, way, u, 0)
    for s in range(2):
        total[s] = multiply(s, r)
    for step in range(1, 4):
        for s in range(2):
            for way, u in lanesets:
                share(s, way, u, step)
            total[s] += multiply(s, ring(r - step, 8)) + multiply(s, ring(r + step, 8))

    last = ring(r + 4, 8)
    summed, sent = {}, {}
    for s in range(2):
        share(s, 0, 0, 4)
        share(s, 1, 1, 4)
        sent[s] = []
        for i in (2, 1, 3, 0):
            peer = ring(k + i, 4)
            rows = pl.ds(pl.multiple_of(peer * 256, 256), 256)
            value = total[s, rows] + dot(held[last, rows], power[s, last], ((1,), (1,)))
            if i:
                b_out[s, i - 1] = value.astype(BF16)
                copy = send(
                    b_out.at[s, i - 1], b_in.at[s, i - 1], b_send.at[s, i - 1], b_recv.at[s, i - 1], {"col": peer}
                )
                sent[s].append((i, copy))
                pending.append(copy)
            else:
                total[s, rows] = value

    swapped = {}
    for s in range(2):
        value = total[s, pl.ds(pl.multiple_of(k * 256, 256), 256)]
        for i, copy in sent[s]:
            copy.wait_recv()
            value = value + b_in[s, i - 1].astype(F32)
        c_out[s] = value.astype(BF16).reshape(2, 128, 128)
        swapped[s] = []
        for i in (4, 3, 5, 2, 6, 1, 7):
            peer = ring(c + i, 8)
            copy = send(
                c_out.at[s, lax.rem(peer, 2)], c_in.at[s, c], c_send.at[s, i - 1], c_recv.at[s, i - 1], {"child": peer}
            )
            swapped[s].append(copy)
            pending.append(copy)
        c_in[s, c] = c_out[s, core]

    spot = 8 * r + 2 * k + core
    offset = 2 * k + core
    gathered = {}
    for s in range(2):
        for copy in swapped[s]:
            copy.wait_recv()
        value = jnp.zeros((128, 128), F32)
        for child in range(8):
            wanted = lax.shift_right_logical(block_map[child, spot], 3) == 4 * r + pair
            value = value + c_in[s, child].astype(F32) * jnp.where(wanted, 1.0, 0.0)
        own_out[:, pl.ds(128 * s, 128)] = value
        z_all[s, offset] = value.astype(BF16)
        gathered[s] = []
        ref = z_all.at[s, offset]
        for i in (2, 1, 3, 0):
            for other in range(2):
                if i == 0 and other == 0:
                    continue
                slot = 2 * i + other
                copy = send(
                    ref, ref, z_send.at[s, slot], z_recv.at[s, slot],
                    {"child": c if other == 0 else 2 * pair + 1 - core, "col": ring(k + i, 4)},
                )
                gathered[s].append(copy)
                pending.append(copy)
    for copy in gathered[0]:
        copy.wait_recv()
    first = z_all[0].reshape(1024, 128)
    gram_out[0] = dot(first, first, ((0,), (0,)))
    yield
    for copy in gathered[1]:
        copy.wait_recv()
    second = z_all[1].reshape(1024, 128)
    gram_out[1] = dot(second, first, ((0,), (0,)))
    gram_out[2] = dot(second, second, ((0,), (0,)))
    for copy in pending:
        copy.wait_send()


def coupling_steps(
    sampling, own, gram, block_map, basis_out, coupling_out,
    held, inverse, corner, front, b_own, e_low, e_high, mine, column_in, row_in, total, sums,
    f_out, f_in, x_out, x_in, g_out, g_in, v_sum, v_out, v_in, h_out, h_in,
    e_send, e_recv, z_send, z_recv, y_send, y_recv, r_send, r_recv, f_send, f_recv, x_send, x_recv,
    g_send, g_recv, v_send, v_recv, h_send, h_recv,
):
    c, r, k = place()
    below, above = {"row": ring(r - 1, 8)}, {"row": ring(r + 1, 8)}
    pending = []
    outgoing = {}
    e_in = (e_low, e_high)

    def spread(s):
        outgoing[s] = []
        for i in (4, 3, 5, 2, 6, 1, 7):
            copy = send(
                b_own.at[s], e_in[s].at[c], e_send.at[s, i - 1], e_recv.at[s, i - 1], {"child": ring(c + i, 8)}
            )
            outgoing[s].append(copy)
            pending.append(copy)
        e_in[s][c] = b_own[s]

    def select(s):
        for copy in outgoing[s]:
            copy.wait_recv()
        for half in range(2):
            near = lax.rem(lax.shift_right_logical(block_map[c, 8 * r + 2 * k + half], 3), 4)
            mine[s, r, pl.ds(128 * half, 128)] = e_in[s][2 * near + half]

    arriving = {}
    forwards = []
    lanesets = ((0, 0), (1, 1), (0, 1), (1, 0))

    def across(s, rel, half):
        chunk = ring(r + rel, 8)
        peer = lax.div(chunk, 2)
        copy = pltpu.make_async_remote_copy(
            src_ref=mine.at[s, chunk, pl.ds(128 * half, 128)],
            dst_ref=column_in.at[s, lax.rem(chunk, 2), k, pl.ds(128 * half, 128)],
            send_sem=y_send.at[s, rel, half],
            recv_sem=y_recv.at[s, lax.rem(chunk, 2), k, half],
            device_id={"col": peer},
            device_id_type=MESH,
        )
        pl.when(peer != k)(copy.start)
        forwards.append((peer, copy))

    def share(s, step):
        for way, half in lanesets:
            hops = 4 - half if way == 0 else 3 + half
            if step > hops:
                continue
            if step:
                arriving[s, way, half, step - 1].wait_recv()
            if step < hops:
                chunk = ring(r - step if way == 0 else r + step, 8)
                ref = mine.at[s, chunk, pl.ds(128 * half, 128)]
                copy = send(
                    ref, ref, z_send.at[s, way, half, step], z_recv.at[s, way, half, step],
                    above if way == 0 else below,
                )
                arriving[s, way, half, step] = copy
                pending.append(copy)
            if step:
                across(s, (8 - step if way == 0 else step) % 8, half)

    row_copies = []

    def rows_out(s):
        for i in (2, 1, 3):
            copy = send(
                mine.at[s, r], row_in.at[s, k], r_send.at[s, i - 1], r_recv.at[s, i - 1], {"col": ring(k + i, 4)}
            )
            row_copies.append(copy)
            pending.append(copy)
        row_in[s, k] = mine[s, r]

    def write_basis(s):
        basis_out[s] = e_in[s][...]

    def weigh_own(s):
        total[s] = dot(held[k], mine[s, 2 * k]) + dot(held[4 + k], mine[s, 2 * k + 1])

    def weigh(s):
        for copy in row_copies[3 * s : 3 * s + 3]:
            copy.wait_recv()
        for i in (1, 3, 2):
            peer = ring(k + i, 4)
            for odd in range(2):
                @pl.when(2 * k + odd == r)
                def _():
                    column_in[s, odd, peer] = row_in[s, peer]

                for half in range(2):
                    arrival = pltpu.make_async_remote_copy(
                        src_ref=mine.at[s, 0, pl.ds(128 * half, 128)],
                        dst_ref=column_in.at[s, odd, peer, pl.ds(128 * half, 128)],
                        send_sem=y_send.at[s, 0, half],
                        recv_sem=y_recv.at[s, odd, peer, half],
                        device_id={"col": peer},
                        device_id_type=MESH,
                    )
                    pl.when(2 * k + odd != r)(arrival.wait_recv)
            total[s] += dot(held[peer], column_in[s, 0, peer]) + dot(held[4 + peer], column_in[s, 1, peer])

    def factor(value, part, actions):
        rows, marks = row_blocks(value), row_blocks(identity(1.0))
        for i in inverse_factor(rows, marks):
            if i in actions:
                actions[i]()
        for t in range(16):
            inverse[part, pl.ds(8 * t, 8)] = marks[t]

    factor(gram[0] + identity(SHIFT), 0, {})
    front[...] = dot(own[:, :128], inverse[0], ((1,), (1,)), HIGHEST)
    b_own[0] = front[...].astype(BF16)
    spread(0)
    for _ in sampling:
        pass
    corner[...] = dot(gram[1], inverse[0], ((1,), (1,)), HIGHEST)

    def begin():
        select(0)
        share(0, 0)
        rows_out(0)

    def relay():
        share(0, 1)

    factor(
        gram[2] + identity(SHIFT) - dot(corner[...], corner[...], ((1,), (1,)), HIGHEST), 1, {10: begin, 15: relay}
    )
    rest = own[:, 128:] - dot(front[...], corner[...], ((1,), (1,)), HIGHEST)
    b_own[1] = dot(rest, inverse[1], ((1,), (1,)), HIGHEST).astype(BF16)
    spread(1)
    share(0, 2)
    write_basis(0)
    select(1)
    share(1, 0)
    rows_out(1)
    share(0, 3)
    share(1, 1)
    share(0, 4)
    share(1, 2)
    write_basis(1)
    share(1, 3)
    weigh_own(0)
    share(1, 4)
    weigh_own(1)
    weigh(0)
    weigh(1)

    sums[...] = jnp.zeros_like(sums)
    for offset in range(8):
        rows = pl.ds(128 * offset, 128)
        value = jnp.concatenate([total[0, rows], total[1, rows]], axis=1)
        high = value.astype(BF16)
        low = (value - high.astype(F32)).astype(BF16)
        spot = pl.ds(128 * (offset % 2), 128)
        left = jnp.concatenate([row_in[0, offset // 2, spot], row_in[1, offset // 2, spot]], axis=1)
        product = dot(left, high, ((0,), (0,))) + dot(left, low, ((0,), (0,)))
        near = lax.rem(lax.shift_right_logical(block_map[c, 8 * r + offset], 3), 4)
        for g in range(4):
            sums[g] += product * jnp.where(near == g, 1.0, 0.0)

    for g in range(2):
        quarters = sums[2 + g].astype(BF16).reshape(4, 4, 16, 256)
        for q in range(4):
            x_out[4 * g + q] = quarters[:, q]
    x_copies, copies = [], []
    for i in (2, 1, 3):
        peer = ring(k + i, 4)
        rows = pl.ds(pl.multiple_of(peer * 64, 64), 64)
        f_out[i - 1] = sums[:2, rows].astype(BF16)
        copies.append(send(f_out.at[i - 1], f_in.at[i - 1], f_send.at[i - 1], f_recv.at[i - 1], {"col": peer}))
    for i in (4, 3, 5, 2, 6, 1, 7):
        peer = ring(c + i, 8)
        x_copies.append(send(x_out.at[peer], x_in.at[c], x_send.at[i - 1], x_recv.at[i - 1], {"child": peer}))
    x_in[c] = x_out[c]
    value = sums[:2, pl.ds(pl.multiple_of(k * 64, 64), 64)]
    for copy, i in zip(copies, (2, 1, 3)):
        copy.wait_recv()
        value = value + f_in[i - 1].astype(F32)
    pending += copies
    g_out[...] = value.astype(BF16).reshape(8, 16, 256)
    g_copies = []
    for i in (4, 3, 5, 2, 6, 1, 7):
        peer = ring(c + i, 8)
        g_copies.append(send(g_out.at[peer], g_in.at[c], g_send.at[i - 1], g_recv.at[i - 1], {"child": peer}))
    g_in[c] = g_out[c]
    for copy in x_copies:
        copy.wait_recv()
    pending += x_copies
    v_sum[...] = jnp.sum(x_in[...].astype(F32), axis=0)
    v_out[...] = v_sum[...].astype(BF16)
    copies = []
    for i in (2, 1, 3):
        peer = ring(k + i, 4)
        copies.append(send(v_out.at[peer], v_in.at[i - 1], v_send.at[i - 1], v_recv.at[i - 1], {"col": peer}))
    for copy in g_copies:
        copy.wait_recv()
    pending += g_copies
    h_out[0] = jnp.sum(g_in[...].astype(F32), axis=0).astype(BF16)
    value = v_sum[k]
    for copy, i in zip(copies, (2, 1, 3)):
        copy.wait_recv()
        value = value + v_in[i - 1].astype(F32)
    pending += copies
    h_out[1] = value.astype(BF16)
    copies = []
    for i in (4, 3, 5, 2, 6, 1, 7):
        copies.append(send(h_out, h_in.at[c], h_send.at[i - 1], h_recv.at[i - 1], {"child": ring(c + i, 8)}))
    h_in[c] = h_out[...]
    for copy in copies:
        copy.wait_recv()
    pending += copies
    coupling_out[...] = h_in[...]
    for copy in pending:
        copy.wait_send()
    for peer, copy in forwards:
        pl.when(peer != k)(copy.wait_send)


def whole_kernel(schur, sketch, block_map, basis_out, coupling_out, own, gram, held, *rest):
    sampling = sample_steps(schur, sketch, block_map, own, gram, held, *rest[:22])
    next(sampling)
    coupling_steps(sampling, own, gram, block_map, basis_out, coupling_out, held, *rest[22:])


def in_vmem():
    return pl.BlockSpec(memory_space=pltpu.VMEM)


def in_smem():
    return pl.BlockSpec(memory_space=pltpu.SMEM)


def solved(schur, sketch, block_map):
    dma = pltpu.SemaphoreType.DMA
    return pl.pallas_call(
        whole_kernel,
        out_shape=(
            jax.ShapeDtypeStruct((2, 8, 128, 128), BF16),
            jax.ShapeDtypeStruct((8, 2, 16, 256), BF16),
        ),
        in_specs=[pl.BlockSpec(memory_space=pl.ANY), in_vmem(), in_smem()],
        out_specs=(in_vmem(), in_vmem()),
        scratch_shapes=[
            pltpu.VMEM((128, 256), F32),
            pltpu.VMEM((3, 128, 128), F32),
            pltpu.VMEM((8, 1024, 256), BF16),
            pltpu.VMEM((256, 1024), BF16),
            pltpu.VMEM((8, 256, 256), F32),
            pltpu.VMEM((2, 2, 2, 4, 64, 256), BF16),
            pltpu.VMEM((2, 2, 2, 4, 64, 256), BF16),
            pltpu.VMEM((2, 8, 128, 256), BF16),
            pltpu.VMEM((2, 1024, 128), F32),
            pltpu.VMEM((2, 3, 256, 128), BF16),
            pltpu.VMEM((2, 3, 256, 128), BF16),
            pltpu.VMEM((2, 2, 128, 128), BF16),
            pltpu.VMEM((2, 8, 128, 128), BF16),
            pltpu.VMEM((2, 8, 128, 128), BF16),
            dma((8,)),
            dma((2, 2, 2, 4)), dma((2, 2, 2, 4)),
            dma((2, 2, 2, 4)), dma((2, 2, 2, 4)),
            dma((2, 3)), dma((2, 3)),
            dma((2, 7)), dma((2, 7)),
            dma((2, 8)), dma((2, 8)),
            pltpu.VMEM((2, 128, 128), F32),
            pltpu.VMEM((128, 128), F32),
            pltpu.VMEM((128, 128), F32),
            pltpu.VMEM((2, 128, 128), BF16),
            pltpu.VMEM((8, 128, 128), BF16),
            pltpu.VMEM((8, 128, 128), BF16),
            pltpu.VMEM((2, 8, 256, 128), BF16),
            pltpu.VMEM((2, 2, 4, 256, 128), BF16),
            pltpu.VMEM((2, 4, 256, 128), BF16),
            pltpu.VMEM((2, 1024, 128), F32),
            pltpu.VMEM((4, 256, 256), F32),
            pltpu.VMEM((3, 2, 64, 256), BF16),
            pltpu.VMEM((3, 2, 64, 256), BF16),
            pltpu.VMEM((8, 4, 16, 256), BF16),
            pltpu.VMEM((8, 4, 16, 256), BF16),
            pltpu.VMEM((8, 16, 256), BF16),
            pltpu.VMEM((8, 16, 256), BF16),
            pltpu.VMEM((4, 16, 256), F32),
            pltpu.VMEM((4, 16, 256), BF16),
            pltpu.VMEM((3, 16, 256), BF16),
            pltpu.VMEM((2, 16, 256), BF16),
            pltpu.VMEM((8, 2, 16, 256), BF16),
            dma((2, 7)), dma((2, 7)),
            dma((2, 2, 2, 4)), dma((2, 2, 2, 4)),
            dma((2, 8, 2)), dma((2, 2, 4, 2)),
            dma((2, 3)), dma((2, 3)),
            dma((3,)), dma((3,)),
            dma((7,)), dma((7,)),
            dma((7,)), dma((7,)),
            dma((3,)), dma((3,)),
            dma((7,)), dma((7,)),
        ],
        compiler_params=pltpu.CompilerParams(
            collective_id=0, has_side_effects=True, vmem_limit_bytes=VMEM_LIMIT
        ),
        name="basis_step",
    )(schur, sketch, block_map)


def place_kernel(basis, coupling, owner_slot, basis_out, coupling_out):
    c, r = lax.axis_index("child"), lax.axis_index("row")
    for slot in range(2):
        share = [jnp.where(owner_slot[4 * r + g] == 2 * c + slot, 1.0, 0.0) for g in range(4)]
        for half in range(2):
            for s in range(2):
                value = basis[s, half].astype(F32) * share[0]
                for g in range(1, 4):
                    value = value + basis[s, 2 * g + half].astype(F32) * share[g]
                basis_out[slot, 0, pl.ds(128 * half, 128), pl.ds(128 * s, 128)] = value
        for q in range(4):
            value = coupling[q, 0].astype(F32) * share[0]
            for g in range(1, 4):
                value = value + coupling[4 * (g % 2) + q, g // 2].astype(F32) * share[g]
            coupling_out[slot, 0, pl.ds(16 * q, 16)] = value


def placed_results(basis, coupling, owner_slot):
    return pl.pallas_call(
        place_kernel,
        out_shape=(
            jax.ShapeDtypeStruct((2, 1, 256, 256), F32),
            jax.ShapeDtypeStruct((2, 1, 64, 256), F32),
        ),
        in_specs=[in_vmem(), in_vmem(), in_smem()],
        out_specs=(in_vmem(), in_vmem()),
        name="results",
    )(basis, coupling, owner_slot)


def shards(schur_blocks, sketch_cols, block_map, owner_slot):
    basis, coupling = solved(schur_blocks, sketch_cols, block_map)
    return placed_results(basis, coupling, owner_slot)


def solution(mesh):
    placed = (P("child", "row", "col"), P("row", None), P(), P())
    return jax.shard_map(
        shards,
        mesh=mesh,
        in_specs=placed,
        out_specs=(P("child", "row", "col", None), P("child", "row", "col", None)),
        check_vma=False,
    )
```
